512 devices in a mesh: seq: 16 (over y, core), kv: 8 (over z), dp: 4 (over x).
Axes of the slice: x: 4, y: 8, z: 8, core: 2. Of those that a mesh axis runs over, the one named last changes fastest.
Arguments:
- queries: bfloat16 [65536, 2048], P(('dp', 'seq', 'kv')), parts along dimension 0, may hold values from -9 to 9
- keys: bfloat16 [65536, 512], P(('dp', 'seq', 'kv')), parts along dimension 0, may hold values from -4 to 4
- values: bfloat16 [65536, 512], P(('dp', 'seq', 'kv')), parts along dimension 0, may hold values from -6 to 6
- doc_ids: int32 [65536], P(('dp', 'seq', 'kv')), parts along dimension 0, may hold values from 0 to 7, never falling along the last dimension, each value on 1 to 4096 neighbouring positions
- beta: float32 [16], replicated, may hold values from -2 to 2
- lin_gain: float32 [2048], replicated, may hold values from 0.1 to 1.9
Outputs:
- mixed: float32 [65536, 2048], P(('dp', 'seq', 'kv')), parts along dimension 0
The draws below stay inside these ranges and needn't reach their ends.
There are 4 independent parts, one for each index of `dp`. The reference program is written for one: setup_inputs(seed, part) draws one part's arguments, and reference() takes and returns one part's arrays. A program takes and returns all parts, laid end to end along the dimension named above; an argument that names none is the same for every part. Nothing has to cross between parts.
Inputs may be any that keep to these rules, and one draw needn't show every extreme that they name: `doc_ids`: document ids never fall along a packed sequence; each document holds 1 to 4096 tokens.
All inputs are finite; a program needn't handle non-finite values.
Results may differ from the reference program's by a relative error of at most 0.0012.
Values may be sent and summed in bfloat16 or wider, within the bound.
A program may use at most 64 MiB of HBM per device.

```python
import math
import jax
import jax.numpy as jnp
import numpy as np
from jax import lax

HEADS = 16
KV_HEADS = 4
HEAD_DIM = 128
DOCS = 8
SEG = 1024
TOKENS = 16384
DOC_MOST = 4096


def draw_keys(key, part):
    shape = (TOKENS, KV_HEADS * HEAD_DIM)
    base = jnp.clip(jax.random.normal(jax.random.fold_in(key, 3), shape, jnp.float32), -4.0, 4.0)
    return base.astype(jnp.bfloat16)


def draw_queries(key, part):
    shape = (TOKENS, HEADS * HEAD_DIM)
    base = jnp.clip(jax.random.normal(jax.random.fold_in(key, 5), shape, jnp.float32), -4.0, 4.0)
    return base.astype(jnp.bfloat16)


def shard_levels(own_key, shape, split, smallest, high):
    def one(position, blocks):
        heights = jax.random.uniform(jax.random.fold_in(jax.random.fold_in(own_key, 6), position), (blocks,), jnp.float32, smallest / len(split), high / len(split))
        return jnp.repeat(jnp.exp(heights), shape[position] // blocks).reshape((-1,) + (1,) * (len(shape) - position - 1))

    level = one(*split[0])
    for cut in split[1:]:
        level = level * one(*cut)
    return level


def length_profile(number_of, total, reach, skew):
    weights = [(1 << 20) // math.isqrt(rank ** skew) + 1 for rank in range(2, number_of + 1)]
    spare, given = total - reach - (number_of - 1), [1] * (number_of - 1)
    while spare > 0:
        movable = [i for i in range(number_of - 1) if given[i] < reach]
        whole, remaining = sum([weights[i] for i in movable]), spare
        for i in movable:
            more = min(reach - given[i], max(1, remaining * weights[i] // whole), spare)
            given[i] = given[i] + more
            spare = spare - more
    return np.array([reach] + given)


def ragged_sizes(rng, amount, total, bound, skew):
    if amount == 2:
        one = jax.random.randint(rng, (), max(1, total - bound), min(bound, total - 1) + 1)
        return jnp.stack([one, total - one])
    sizes = jnp.asarray(length_profile(amount, total, bound, skew), jnp.int32)
    pairs = (amount - 1) // 2
    giver, receiver = sizes[1:1 + 2 * pairs:2], sizes[2:2 + 2 * pairs:2]
    room = jnp.minimum(giver - 1, bound - receiver)
    moved = jax.random.randint(jax.random.fold_in(rng, 1), (pairs,), 0, 1 << 20) % (room + 1)
    sizes = sizes.at[1:1 + 2 * pairs:2].set(giver - moved).at[2:2 + 2 * pairs:2].set(receiver + moved)
    return sizes[jax.random.permutation(jax.random.fold_in(rng, 2), amount)]


def noise(key, shape, scale, bound, shards=(), held_as=jnp.bfloat16):
    result = scale * jax.random.normal(key, shape, jnp.float32)
    if shards:
        result = result * shard_levels(key, shape, shards, -0.22, 0.18)
    return jnp.clip(result, -bound, bound).astype(held_as)


def setup_inputs(seed: int = 0, part: int = 0) -> dict:
    arg_keys = jax.random.split(jax.random.key(seed), 7)
    own_keys = jax.random.split(jax.random.fold_in(arg_keys[6], part), 7)
    queries = draw_queries(jax.random.fold_in(jax.random.fold_in(arg_keys[6], part), 71), part)
    keys = draw_keys(jax.random.fold_in(jax.random.fold_in(arg_keys[6], part), 71), part)
    values = noise(own_keys[2], (TOKENS, KV_HEADS * HEAD_DIM), 1.0, 6.0, ((0, 128),))
    doc_ids = jnp.searchsorted(jnp.cumsum(ragged_sizes(own_keys[3], DOCS, TOKENS, DOC_MOST, 1)), jnp.arange(TOKENS), side="right").astype(jnp.int32)
    beta = jnp.clip(jax.random.uniform(arg_keys[4], (HEADS,), jnp.float32, -2.0, 2.0), -2.0, 2.0)
    lin_gain = jnp.clip(1.0 + 0.18 * jax.random.normal(arg_keys[5], (HEADS * HEAD_DIM,), jnp.float32), 0.1, 1.9)
    return dict(queries=queries, keys=keys, values=values, doc_ids=doc_ids, beta=beta, lin_gain=lin_gain)


def reference(queries, keys, values, doc_ids, beta, lin_gain):
    groups = HEADS // KV_HEADS
    segments = TOKENS // SEG
    query_heads = queries.reshape(segments, SEG, KV_HEADS, groups, HEAD_DIM)
    key_heads = keys.reshape(segments, SEG, KV_HEADS, HEAD_DIM)
    value_heads = values.reshape(segments, SEG, KV_HEADS, HEAD_DIM)
    seg_docs = doc_ids.reshape(segments, SEG)

    def memory_step(carry, item):
        state, last_doc = carry
        seg_queries, seg_keys, seg_values, docs_here = item
        live = (docs_here == last_doc).astype(jnp.float32)
        recalled = jnp.einsum('sgqd,gde->sgqe', seg_queries.astype(jnp.float32), state, precision=lax.Precision.HIGHEST)
        recalled = recalled * live[:, None, None, None]
        tail = (docs_here == docs_here[-1]).astype(jnp.float32)
        part_state = jnp.einsum('sgd,sge->gde', seg_keys.astype(jnp.float32) * tail[:, None, None], seg_values.astype(jnp.float32), precision=lax.Precision.HIGHEST)
        joined = (docs_here[0] == docs_here[-1]) & (last_doc == docs_here[-1])
        new_state = part_state + jnp.where(joined, state, jnp.zeros_like(state))
        return ((new_state, docs_here[-1]), recalled)
    initial = (jnp.zeros((KV_HEADS, HEAD_DIM, HEAD_DIM), jnp.float32), jnp.array(-1, jnp.int32))
    _, recalled = lax.scan(memory_step, initial, (query_heads, key_heads, value_heads, seg_docs))
    mean_square = lax.optimization_barrier(jnp.mean(recalled * recalled, axis=-1, keepdims=True))
    normed = recalled * lax.rsqrt(mean_square + 1e-06) * lin_gain.reshape(KV_HEADS, groups, HEAD_DIM)

    def attend(item):
        seg_queries, seg_keys, seg_values, docs_here = item
        scores = jnp.einsum('sgqd,tgd->gqst', seg_queries.astype(jnp.float32), seg_keys.astype(jnp.float32)) / jnp.sqrt(jnp.float32(HEAD_DIM))
        places = jnp.arange(SEG, dtype=jnp.int32)
        allowed = (places[None, :] <= places[:, None]) & (docs_here[None, :] == docs_here[:, None])
        masked = jnp.where(allowed, scores, jnp.float32(-1e+30))
        row_max = lax.optimization_barrier(jnp.max(masked, axis=-1, keepdims=True))
        expos = jnp.where(allowed, jnp.exp(masked - row_max), jnp.float32(0.0))
        total = lax.optimization_barrier(jnp.sum(expos, axis=-1))
        weights = expos.astype(jnp.bfloat16)
        summed = jnp.einsum('gqst,tge->sgqe', weights.astype(jnp.float32), seg_values.astype(jnp.float32))
        return summed / jnp.transpose(total, (2, 0, 1))[..., None]
    attended = lax.map(attend, (query_heads, key_heads, value_heads, seg_docs))
    mixing = jax.nn.sigmoid(beta).reshape(KV_HEADS, groups)[None, None, :, :, None]
    mixed = mixing * normed + (1.0 - mixing) * attended
    return mixed.reshape(TOKENS, HEADS * HEAD_DIM).astype(jnp.float32)
```

```python
import functools
import math

import jax
import jax.numpy as jnp
from jax import lax
from jax.experimental import pallas as pl
from jax.experimental.pallas import tpu as pltpu
from jax.sharding import PartitionSpec as P

HEADS = 16
GROUPS = 4
D = 128
MESH = pl.DeviceIdType.MESH
F32 = jnp.float32
BF16 = jnp.bfloat16
HOPS = (4, 3, 3, 4)


def kernel(n_kv, n_seq, rows, q_hbm, k_hbm, v_hbm, docs_ref, beta_ref, gain_ref, out_hbm,
           q_vm, k_vm, kb, vb, docs, bias, tail, att, t_own, t_oth, c_own, c_in,
           in_sem, out_sem, ring_send, ring_recv, doc_send, doc_recv, st_send, st_recv):
    me = lax.axis_index("kv")
    seq = lax.axis_index("seq")
    right, left = lax.rem(me + 1, n_kv), lax.rem(me + n_kv - 1, n_kv)
    core = lax.rem(seq, 2)
    other = seq + 1 - 2 * core
    chip = seq // 2

    def along(step):
        return lax.rem(seq + 2 * step + n_seq, n_seq)

    def k_in(g):
        return pltpu.make_async_copy(k_hbm.at[:, pl.ds(g * D, D)], k_vm.at[g], in_sem.at[g])

    def v_in(g):
        return pltpu.make_async_copy(v_hbm.at[:, pl.ds(g * D, D)], vb.at[g, me], in_sem.at[GROUPS + g])

    def q_in(h):
        cols = pl.ds(pl.multiple_of(h * D, D), D)
        return pltpu.make_async_copy(q_hbm.at[:, cols], q_vm.at[h], in_sem.at[2 * GROUPS + h])

    barrier = pltpu.get_barrier_semaphore()
    for d in range(1, n_kv):
        pl.semaphore_signal(barrier, inc=1, device_id={"kv": lax.rem(me + d, n_kv)}, device_id_type=MESH)
    for s in (other, along(1), along(2), along(-1), along(-2)):
        pl.semaphore_signal(barrier, inc=1, device_id={"seq": s}, device_id_type=MESH)
    for g in range(GROUPS):
        k_in(g).start()
        v_in(g).start()

    @pl.loop(0, HEADS)
    def _(h):
        q_in(h).start()

    docs[me] = jnp.broadcast_to(docs_ref[...], (8, rows))
    for g in range(GROUPS):
        k_in(g).wait()
        kb[g, me] = k_vm[g].T
    for g in range(GROUPS):
        v_in(g).wait()
    pl.semaphore_wait(barrier, n_kv - 1 + 5)

    def doc_copy(d):
        return pltpu.make_async_remote_copy(
            src_ref=docs.at[me], dst_ref=docs.at[me],
            send_sem=doc_send.at[d - 1], recv_sem=doc_recv.at[d - 1],
            device_id={"kv": lax.rem(me + d, n_kv)}, device_id_type=MESH)

    def doc_arrival(d):
        src = lax.rem(me - d + n_kv, n_kv)
        return pltpu.make_async_remote_copy(
            src_ref=docs.at[src], dst_ref=docs.at[src],
            send_sem=doc_send.at[d - 1], recv_sem=doc_recv.at[d - 1],
            device_id={"kv": lax.rem(me + d, n_kv)}, device_id_type=MESH)

    def ring(t, g, h):
        buf = kb if t < 2 else vb
        onward = t % 2 == 0
        blk = lax.rem(me - h + n_kv, n_kv) if onward else lax.rem(me + h, n_kv)
        return pltpu.make_async_remote_copy(
            src_ref=buf.at[g, blk], dst_ref=buf.at[g, blk],
            send_sem=ring_send.at[t, g, h], recv_sem=ring_recv.at[t, g, h],
            device_id={"kv": right if onward else left}, device_id_type=MESH)

    def arrival(t, g, h):
        buf = kb if t < 2 else vb
        onward = t % 2 == 0
        blk = lax.rem(me - h - 1 + n_kv, n_kv) if onward else lax.rem(me + h + 1, n_kv)
        return pltpu.make_async_remote_copy(
            src_ref=buf.at[g, blk], dst_ref=buf.at[g, blk],
            send_sem=ring_send.at[t, g, h], recv_sem=ring_recv.at[t, g, h],
            device_id={"kv": right if onward else left}, device_id_type=MESH)

    def first_sends(g):
        for t in range(4):
            ring(t, g, 0).start()

    def hop(g, h):
        for t in range(4):
            if h < HOPS[t]:
                arrival(t, g, h).wait_recv()
                if h + 1 < HOPS[t]:
                    ring(t, g, h + 1).start()

    def state_to_other(g):
        return pltpu.make_async_remote_copy(
            src_ref=t_own.at[g], dst_ref=t_oth.at[g],
            send_sem=st_send.at[0, g], recv_sem=st_recv.at[0, g],
            device_id={"seq": other}, device_id_type=MESH)

    def state_along(g, step):
        return pltpu.make_async_remote_copy(
            src_ref=c_own.at[g], dst_ref=c_in.at[step - 1, g],
            send_sem=st_send.at[step, g], recv_sem=st_recv.at[step, g],
            device_id={"seq": along(step)}, device_id_type=MESH)

    first_sends(0)
    for d in range(1, n_kv):
        doc_copy(d).start()
    for d in range(1, n_kv):
        doc_arrival(d).wait_recv()

    own_doc = jnp.broadcast_to(docs_ref[...].astype(F32), (rows, rows)).T
    row = lax.broadcasted_iota(jnp.int32, (rows, rows), 0)
    lane = lax.broadcasted_iota(jnp.int32, (rows, rows), 1)
    last_doc = jnp.max(docs[n_kv - 1].astype(F32), axis=1, keepdims=True)[0:1]
    first_doc = jnp.min(docs[0].astype(F32), axis=1, keepdims=True)[0:1]
    for j in range(n_kv):
        doc_j = docs[j, 0:1].astype(F32)
        allowed = (doc_j == own_doc) & (j * rows + lane <= me * rows + row)
        bias[:, j * rows:(j + 1) * rows] = jnp.where(allowed, 0.0, -1e30)
        tail[:, j * rows:(j + 1) * rows] = jnp.broadcast_to(
            jnp.where(doc_j == last_doc, 1.0, 0.0), (8, rows))
    live = jnp.where(own_doc[:, 0:1] == first_doc, 1.0, 0.0)

    @pl.loop(0, HEADS)
    def _(h):
        q_in(h).wait()

    scale = math.log2(math.e) / math.sqrt(D)

    def mixing(h):
        return jax.nn.sigmoid(jnp.full((1, D), beta_ref[h], F32))

    def attend(g, pair):
        h0 = 4 * g + 2 * pair
        q2 = jnp.concatenate([q_vm[h0], q_vm[h0 + 1]], axis=0)
        kt = jnp.concatenate([kb[g, j] for j in range(n_kv)], axis=1)
        s = jnp.dot(q2, kt, preferred_element_type=F32)
        b = bias[...]
        s = s + jnp.concatenate([b, b], axis=0)
        m = jnp.max(s, axis=-1, keepdims=True)
        p = jnp.exp2((s - m) * scale)
        total = jnp.sum(p, axis=-1, keepdims=True)
        o = jnp.dot(p.astype(BF16), vb[g].reshape(n_kv * rows, D), preferred_element_type=F32)
        o = o / total
        att[h0] = o[:rows] * (1.0 - mixing(h0))
        att[h0 + 1] = o[rows:] * (1.0 - mixing(h0 + 1))

    def tail_state(g):
        kt = jnp.concatenate([kb[g, j] for j in range(n_kv)], axis=1)
        kt = kt * tail[0:1].astype(BF16)
        t = jnp.dot(kt, vb[g].reshape(n_kv * rows, D), preferred_element_type=F32)
        t_own[g, 0:D] = t
        t_own[g, D:D + 8] = jnp.broadcast_to(last_doc, (8, D))

    def chip_state(g):
        own, oth = t_own[g], t_oth[g]
        even = jnp.where(core == 0, own, oth)
        odd = jnp.where(core == 0, oth, own)
        same = even[D:D + 1] == odd[D:D + 1]
        c_own[g, 0:D] = odd[0:D] + jnp.where(same, even[0:D], 0.0)
        c_own[g, D:D + 8] = odd[D:D + 8]

    def recall(g):
        one, two, near = c_in[0, g], c_in[1, g], t_oth[g]
        mem = jnp.where((one[D:D + 1] == first_doc) & (chip >= 1), one[0:D], 0.0)
        mem = mem + jnp.where((two[D:D + 1] == first_doc) & (chip >= 2), two[0:D], 0.0)
        mem = mem + jnp.where((near[D:D + 1] == first_doc) & (core == 1), near[0:D], 0.0)
        hi = mem.astype(BF16)
        lo = (mem - hi.astype(F32)).astype(BF16)
        both = jnp.concatenate([hi, lo], axis=1)
        q4 = jnp.concatenate([q_vm[4 * g + k] for k in range(4)], axis=0)
        r = jnp.dot(q4, both, preferred_element_type=F32)
        r = r[:, 0:D] + r[:, D:]
        for k in range(4):
            h = 4 * g + k
            rh = r[k * rows:(k + 1) * rows] * live
            mean = jnp.mean(rh * rh, axis=-1, keepdims=True)
            cols = pl.ds(pl.multiple_of(h * D, D), D)
            att[h] = att[h] + rh * lax.rsqrt(mean + 1e-6) * (gain_ref[:, cols] * mixing(h))

    def out_copy(h):
        cols = pl.ds(pl.multiple_of(h * D, D), D)
        return pltpu.make_async_copy(att.at[h], out_hbm.at[:, cols], out_sem.at[h])

    @pl.loop(0, GROUPS + 2)
    def _(n):
        @pl.when(n + 1 < GROUPS)
        def _():
            first_sends(n + 1)

        @pl.when(n >= 2)
        def _():
            g = n - 2
            state_to_other(g).wait_recv()
            chip_state(g)
            state_along(g, 1).start()
            state_along(g, 2).start()

        for half in range(2):
            @pl.when((n >= 1) & (n <= GROUPS))
            def _():
                hop(n - 1, 2 + half)

            @pl.when(n < GROUPS)
            def _():
                hop(n, half)

            if half == 1:
                @pl.when((n >= 1) & (n <= GROUPS))
                def _():
                    tail_state(n - 1)
                    state_to_other(n - 1).start()

            @pl.when(n >= 2)
            def _():
                attend(n - 2, half)

        @pl.when(n >= 2)
        def _():
            g = n - 2
            state_along(g, 1).wait_recv()
            state_along(g, 2).wait_recv()
            recall(g)
            for k in range(4):
                out_copy(4 * g + k).start()

    for d in range(1, n_kv):
        doc_copy(d).wait_send()

    @pl.loop(0, GROUPS)
    def _(g):
        for t in range(4):
            for h in range(HOPS[t]):
                ring(t, g, h).wait_send()
        state_to_other(g).wait_send()
        state_along(g, 1).wait_send()
        state_along(g, 2).wait_send()

    @pl.loop(0, HEADS)
    def _(h):
        out_copy(h).wait()


def on_device(n_kv, n_seq, queries, keys, values, doc_ids, beta, lin_gain):
    rows = queries.shape[0]
    hbm = pl.BlockSpec(memory_space=pl.ANY)
    vmem = pl.BlockSpec(memory_space=pltpu.VMEM)
    smem = pl.BlockSpec(memory_space=pltpu.SMEM)
    dma = pltpu.SemaphoreType.DMA
    return pl.pallas_call(
        functools.partial(kernel, n_kv, n_seq, rows),
        out_shape=jax.ShapeDtypeStruct((rows, HEADS * D), F32),
        in_specs=[hbm, hbm, hbm, vmem, smem, vmem],
        out_specs=hbm,
        scratch_shapes=[
            pltpu.VMEM((HEADS, rows, D), BF16),
            pltpu.VMEM((GROUPS, rows, D), BF16),
            pltpu.VMEM((GROUPS, n_kv, D, rows), BF16),
            pltpu.VMEM((GROUPS, n_kv, rows, D), BF16),
            pltpu.VMEM((n_kv, 8, rows), jnp.int32),
            pltpu.VMEM((rows, n_kv * rows), F32),
            pltpu.VMEM((8, n_kv * rows), F32),
            pltpu.VMEM((HEADS, rows, D), F32),
            pltpu.VMEM((GROUPS, D + 8, D), F32),
            pltpu.VMEM((GROUPS, D + 8, D), F32),
            pltpu.VMEM((GROUPS, D + 8, D), F32),
            pltpu.VMEM((2, GROUPS, D + 8, D), F32),
            dma((2 * GROUPS + HEADS,)),
            dma((HEADS,)),
            dma((4, GROUPS, 4)),
            dma((4, GROUPS, 4)),
            dma((n_kv - 1,)),
            dma((n_kv - 1,)),
            dma((3, GROUPS)),
            dma((3, GROUPS)),
        ],
        compiler_params=pltpu.CompilerParams(
            collective_id=0, has_side_effects=True, vmem_limit_bytes=32 * 1024 * 1024),
    )(queries, keys, values, doc_ids.reshape(1, rows), beta, lin_gain.reshape(1, HEADS * D))


def solution(mesh):
    split = P(("dp", "seq", "kv"))
    rows = P(("dp", "seq", "kv"), None)
    return jax.shard_map(
        functools.partial(on_device, mesh.shape["kv"], mesh.shape["seq"]),
        mesh=mesh, in_specs=(rows, rows, rows, split, P(), P()), out_specs=rows, check_vma=False)
```

```python
import functools
import math

import jax
import jax.numpy as jnp
from jax import lax
from jax.experimental import pallas as pl
from jax.experimental.pallas import tpu as pltpu
from jax.sharding import PartitionSpec as P

HEADS = 16
GROUPS = 4
D = 128
MESH = pl.DeviceIdType.MESH
F32 = jnp.float32
BF16 = jnp.bfloat16
NEG = -1e30
NEAR = (-2, -1, 0, 1, 2)
FAR = (-3, 3, 4)


def kernel(n_kv, n_seq, rows, q_hbm, k_hbm, v_hbm, docs_ref, beta_ref, gain_ref, out_hbm,
           q_vm, k_vm, kv, docs, bias, top, total, acc, att, p_own, p_in, t_own, t_oth, c_own, c_in, x_own, x_in, mem,
           in_sem, out_sem, ring_send, ring_recv, doc_send, doc_recv, p_send, p_recv, st_send, st_recv, mem_send, mem_recv):
    me = lax.axis_index("kv")
    seq = lax.axis_index("seq")
    core = lax.rem(seq, 2)
    other = seq + 1 - 2 * core
    chip = seq // 2
    half = n_kv // 2
    mine = lax.rem(me, GROUPS)

    def away(step):
        return lax.rem(me + step + n_kv, n_kv)

    def along(step):
        return lax.rem(seq + 2 * step + n_seq, n_seq)

    odd_step = 4 * lax.rem(me, 2) - 2
    barrier = pltpu.get_barrier_semaphore()
    for d in range(1, n_kv):
        pl.semaphore_signal(barrier, inc=1, device_id={"kv": away(d)}, device_id_type=MESH)
    for d in (other, along(1), along(2), along(-1), along(-2)):
        pl.semaphore_signal(barrier, inc=1, device_id={"seq": d}, device_id_type=MESH)

    def k_in(g):
        return pltpu.make_async_copy(k_hbm.at[:, pl.ds(g * D, D)], k_vm.at[g], in_sem.at[g])

    def v_in(g):
        return pltpu.make_async_copy(
            v_hbm.at[:, pl.ds(g * D, D)], kv.at[g, me, pl.ds(D, rows)], in_sem.at[GROUPS + g])

    def q_in(h):
        cols = pl.ds(pl.multiple_of(h * D, D), D)
        return pltpu.make_async_copy(q_hbm.at[:, cols], q_vm.at[h], in_sem.at[2 * GROUPS + h])

    for g in range(GROUPS):
        k_in(g).start()
    for g in range(GROUPS):
        v_in(g).start()
    for h in range(HEADS):
        q_in(h).start()
    docs[me] = jnp.broadcast_to(docs_ref[...].astype(BF16), (16, rows))
    for j in range(half, n_kv):
        @pl.when(j > me)
        def _():
            for g in range(GROUPS):
                kv[g, j] = jnp.zeros((D + rows, D), BF16)
    for g in range(GROUPS):
        k_in(g).wait()
        kv[g, me, 0:D] = k_vm[g].T
    own_row = docs_ref[...].astype(F32)
    ending = jnp.where(own_row == jnp.max(own_row, axis=1, keepdims=True), 1.0, 0.0).astype(BF16)
    for g in range(GROUPS):
        v_in(g).wait()
        p_own[g] = jnp.dot(kv[g, me, 0:D] * ending, kv[g, me, D:D + rows], preferred_element_type=F32)
    pl.semaphore_wait(barrier, n_kv - 1 + 5)

    def doc_copy(d, ahead):
        blk = away(-d) if ahead else me
        return pltpu.make_async_remote_copy(
            src_ref=docs.at[blk], dst_ref=docs.at[blk],
            send_sem=doc_send.at[d - 1], recv_sem=doc_recv.at[d - 1],
            device_id={"kv": away(d)}, device_id_type=MESH)

    def part_copy(slot):
        step = (1, -1, odd_step)[slot]
        g = lax.rem(me + (1, GROUPS - 1, 2)[slot], GROUPS)
        return pltpu.make_async_remote_copy(
            src_ref=p_own.at[g], dst_ref=p_in.at[slot],
            send_sem=p_send.at[slot], recv_sem=p_recv.at[slot],
            device_id={"kv": away(step)}, device_id_type=MESH)

    def span(h, onward):
        if h < half - 1:
            return pl.ds(0, D + rows)
        return pl.ds(0, D) if onward else pl.ds(D, rows)

    def ring(onward, g, h, ahead):
        blk = away(-h - ahead if onward else h + ahead)
        ref = kv.at[g, blk, span(h, onward)]
        t = 0 if onward else 1
        return pltpu.make_async_remote_copy(
            src_ref=ref, dst_ref=ref, send_sem=ring_send.at[t, g, h], recv_sem=ring_recv.at[t, g, h],
            device_id={"kv": away(1 if onward else -1)}, device_id_type=MESH)

    def sent(h, onward):
        return (me >= h) & (me < n_kv - 1) if onward else away(h) < half

    def arrives(h, onward):
        return me > h if onward else away(h + 1) < half

    def send(g, h):
        for onward in (True, False):
            @pl.when(sent(h, onward))
            def _():
                ring(onward, g, h, 0).start()

    def hop(g, h):
        for onward in (True, False):
            @pl.when(arrives(h, onward))
            def _():
                ring(onward, g, h, 1).wait_recv()
            if h + 1 < half:
                @pl.when(sent(h + 1, onward))
                def _():
                    ring(onward, g, h + 1, 0).start()

    def state_to_other():
        return pltpu.make_async_remote_copy(
            src_ref=t_own, dst_ref=t_oth, send_sem=st_send.at[0], recv_sem=st_recv.at[0],
            device_id={"seq": other}, device_id_type=MESH)

    def state_along(step):
        return pltpu.make_async_remote_copy(
            src_ref=c_own, dst_ref=c_in.at[step - 1], send_sem=st_send.at[step], recv_sem=st_recv.at[step],
            device_id={"seq": along(step)}, device_id_type=MESH)

    def state_across():
        return pltpu.make_async_remote_copy(
            src_ref=x_own, dst_ref=x_in, send_sem=st_send.at[3], recv_sem=st_recv.at[3],
            device_id={"kv": away(half)}, device_id_type=MESH)

    def memory_out(slot):
        target = away((1, -1, odd_step)[slot])
        return pltpu.make_async_remote_copy(
            src_ref=mem.at[mine], dst_ref=mem.at[mine],
            send_sem=mem_send.at[slot], recv_sem=mem_recv.at[slot],
            device_id={"kv": target}, device_id_type=MESH)

    def memory_in(slot):
        g = lax.rem(me + (GROUPS - 1, 1, 2)[slot], GROUPS)
        return pltpu.make_async_remote_copy(
            src_ref=mem.at[g], dst_ref=mem.at[g],
            send_sem=mem_send.at[slot], recv_sem=mem_recv.at[slot],
            device_id={"kv": away(1)}, device_id_type=MESH)

    own_doc = jnp.broadcast_to(docs_ref[...].astype(F32), (rows, rows)).T

    def doc_row(j):
        return docs[j].astype(F32)[0:1]

    def ends():
        last = jnp.max(doc_row(n_kv - 1), axis=1, keepdims=True)
        first = jnp.min(doc_row(0), axis=1, keepdims=True)
        return first, last

    def masks():
        row = lax.broadcasted_iota(jnp.int32, (rows, rows), 0)
        lane = lax.broadcasted_iota(jnp.int32, (rows, rows), 1)
        for j in range(n_kv):
            allowed = (doc_row(j) == own_doc) & (j * rows + lane <= me * rows + row)
            bias[j] = jnp.where(allowed, 0.0, NEG)

    scale = math.log2(math.e) / math.sqrt(D)

    def mixing(h):
        return jax.nn.sigmoid(jnp.full((1, D), beta_ref[h], F32))

    def scores(i, offs):
        g = i // 2
        q2 = jnp.concatenate([q_vm[2 * i], q_vm[2 * i + 1]], axis=0)
        kt = jnp.concatenate([kv[g, away(o), 0:D] for o in offs], axis=1)
        b = jnp.concatenate([bias[away(o)] for o in offs], axis=1)
        s = jnp.dot(q2, kt, preferred_element_type=F32)
        return s + jnp.concatenate([b, b], axis=0)

    def weighted(i, offs, p):
        v = jnp.concatenate([kv[i // 2, away(o), D:D + rows] for o in offs], axis=0)
        return jnp.dot(p.astype(BF16), v, preferred_element_type=F32)

    def near(i):
        s = scores(i, NEAR)
        m = jnp.max(s, axis=-1, keepdims=True)
        p = jnp.exp2((s - m) * scale)
        top[i] = m
        total[i] = jnp.sum(p, axis=-1, keepdims=True)
        acc[i] = weighted(i, NEAR, p)

    def far(i):
        s = scores(i, FAR)
        old = top[i]
        m = jnp.maximum(old, jnp.max(s, axis=-1, keepdims=True))
        p = jnp.exp2((s - m) * scale)
        kept = jnp.exp2((old - m) * scale)
        norm = total[i] * kept + jnp.sum(p, axis=-1, keepdims=True)
        o = (acc[i] * kept + weighted(i, FAR, p)) / norm
        att[2 * i] = o[:rows] * (1.0 - mixing(2 * i))
        att[2 * i + 1] = o[rows:] * (1.0 - mixing(2 * i + 1))

    def some(f, start, stop):
        pl.loop(start, stop)(f)

    def tail_state():
        for slot in range(3):
            part_copy(slot).wait_recv()
        last_doc = ends()[1]

        def counted(blk, part):
            here = jnp.max(doc_row(blk), axis=1, keepdims=True)
            return jnp.where(here == last_doc, part, 0.0)

        t_own[0:D] = (counted(me, p_own[mine]) + counted(away(-1), p_in[0])
                      + counted(away(1), p_in[1]) + counted(away(-odd_step), p_in[2]))
        t_own[D:D + 8] = jnp.broadcast_to(last_doc, (8, D))
        state_to_other().start()

    def chip_state():
        state_to_other().wait_recv()
        own, oth = t_own[...], t_oth[...]
        even = jnp.where(core == 0, own, oth)
        odd = jnp.where(core == 0, oth, own)
        same = even[D:D + 1] == odd[D:D + 1]
        c_own[0:D] = odd[0:D] + jnp.where(same, even[0:D], 0.0)
        c_own[D:D + 8] = odd[D:D + 8]
        state_along(1).start()
        state_along(2).start()

    def part_memory():
        first_doc = ends()[0]
        state_along(1).wait_recv()
        state_along(2).wait_recv()
        one, two, beside = c_in[0], c_in[1], t_oth[...]
        part = jnp.where((one[D:D + 1] == first_doc) & (chip >= 1), one[0:D], 0.0)
        part = part + jnp.where((two[D:D + 1] == first_doc) & (chip >= 2), two[0:D], 0.0)
        part = part + jnp.where((beside[D:D + 1] == first_doc) & (core == 1), beside[0:D], 0.0)
        x_own[...] = part
        state_across().start()

    def own_memory():
        state_across().wait_recv()
        mem[mine] = x_own[...] + x_in[...]
        for slot in range(3):
            memory_out(slot).start()

    def out_copy(h):
        cols = pl.ds(pl.multiple_of(h * D, D), D)
        return pltpu.make_async_copy(att.at[h], out_hbm.at[:, cols], out_sem.at[h])

    def recall(g):
        live = jnp.where(own_doc[:, 0:1] == ends()[0], 1.0, 0.0)
        state = mem[g]
        hi = state.astype(BF16)
        lo = (state - hi.astype(F32)).astype(BF16)
        both = jnp.concatenate([hi, lo], axis=1)
        q4 = jnp.concatenate([q_vm[4 * g + k] for k in range(4)], axis=0)
        r = jnp.dot(q4, both, preferred_element_type=F32)
        r = r[:, 0:D] + r[:, D:]
        for k in range(4):
            h = 4 * g + k
            rh = r[k * rows:(k + 1) * rows] * live
            mean = jnp.mean(rh * rh, axis=-1, keepdims=True)
            cols = pl.ds(pl.multiple_of(h * D, D), D)
            att[h] = att[h] + rh * lax.rsqrt(mean + 1e-6) * (gain_ref[:, cols] * mixing(h))
            out_copy(h).start()

    for d in range(1, n_kv):
        doc_copy(d, False).start()
    for slot in range(3):
        part_copy(slot).start()
    for g in range(GROUPS):
        send(g, 0)
    for d in range(1, n_kv):
        doc_copy(d, True).wait_recv()
    masks()
    tail_state()
    hop(0, 0)
    chip_state()
    for h in range(HEADS):
        q_in(h).wait()
    hop(1, 0)
    hop(2, 0)
    hop(3, 0)
    hop(0, 1)
    hop(1, 1)
    part_memory()
    some(near, 0, 1)
    hop(2, 1)
    some(near, 1, 3)
    hop(3, 1)
    some(near, 3, 4)
    hop(0, 2)
    some(near, 4, 5)
    own_memory()
    hop(1, 2)
    some(near, 5, 6)
    hop(2, 2)
    some(near, 6, 7)
    hop(3, 2)
    some(near, 7, 8)
    for slot in range(3):
        memory_in(slot).wait_recv()
    hop(0, 3)
    some(far, 0, 2)
    some(recall, 0, 1)
    hop(1, 3)
    some(far, 2, 4)
    some(recall, 1, 2)
    hop(2, 3)
    some(far, 4, 6)
    some(recall, 2, 3)
    hop(3, 3)
    some(far, 6, 8)
    some(recall, 3, 4)

    for h in range(half):
        for onward in (True, False):
            @pl.when(sent(h, onward))
            def _():
                for g in range(GROUPS):
                    ring(onward, g, h, 0).wait_send()
    for d in range(1, n_kv):
        doc_copy(d, False).wait_send()
    for slot in range(3):
        part_copy(slot).wait_send()
    state_to_other().wait_send()
    state_along(1).wait_send()
    state_along(2).wait_send()
    state_across().wait_send()
    for slot in range(3):
        memory_out(slot).wait_send()
    for h in range(HEADS):
        out_copy(h).wait()


def on_device(n_kv, n_seq, queries, keys, values, doc_ids, beta, lin_gain):
    rows = queries.shape[0]
    hbm = pl.BlockSpec(memory_space=pl.ANY)
    vmem = pl.BlockSpec(memory_space=pltpu.VMEM)
    smem = pl.BlockSpec(memory_space=pltpu.SMEM)
    dma = pltpu.SemaphoreType.DMA
    state = pltpu.VMEM((D + 8, D), F32)
    return pl.pallas_call(
        functools.partial(kernel, n_kv, n_seq, rows),
        out_shape=jax.ShapeDtypeStruct((rows, HEADS * D), F32),
        in_specs=[hbm, hbm, hbm, vmem, smem, vmem],
        out_specs=hbm,
        scratch_shapes=[
            pltpu.VMEM((HEADS, rows, D), BF16),
            pltpu.VMEM((GROUPS, rows, D), BF16),
            pltpu.VMEM((GROUPS, n_kv, D + rows, D), BF16),
            pltpu.VMEM((n_kv, 16, rows), BF16),
            pltpu.VMEM((n_kv, rows, rows), F32),
            pltpu.VMEM((HEADS // 2, 2 * rows, 1), F32),
            pltpu.VMEM((HEADS // 2, 2 * rows, 1), F32),
            pltpu.VMEM((HEADS // 2, 2 * rows, D), F32),
            pltpu.VMEM((HEADS, rows, D), F32),
            pltpu.VMEM((GROUPS, D, D), F32),
            pltpu.VMEM((3, D, D), F32),
            state, state, state,
            pltpu.VMEM((2, D + 8, D), F32),
            pltpu.VMEM((D, D), F32),
            pltpu.VMEM((D, D), F32),
            pltpu.VMEM((GROUPS, D, D), F32),
            dma((2 * GROUPS + HEADS,)),
            dma((HEADS,)),
            dma((2, GROUPS, n_kv // 2)),
            dma((2, GROUPS, n_kv // 2)),
            dma((n_kv - 1,)),
            dma((n_kv - 1,)),
            dma((3,)),
            dma((3,)),
            dma((4,)),
            dma((4,)),
            dma((3,)),
            dma((3,)),
        ],
        compiler_params=pltpu.CompilerParams(
            collective_id=0, has_side_effects=True, vmem_limit_bytes=60 * 1024 * 1024),
    )(queries, keys, values, doc_ids.reshape(1, rows), beta, lin_gain.reshape(1, HEADS * D))


def solution(mesh):
    split = P(("dp", "seq", "kv"))
    rows = P(("dp", "seq", "kv"), None)
    return jax.shard_map(
        functools.partial(on_device, mesh.shape["kv"], mesh.shape["seq"]),
        mesh=mesh, in_specs=(rows, rows, rows, split, P(), P()), out_specs=rows, check_vma=False)
```

```python
import functools
import math

import jax
import jax.numpy as jnp
from jax import lax
from jax.experimental import pallas as pl
from jax.experimental.pallas import tpu as pltpu
from jax.sharding import PartitionSpec as P

HEADS = 16
GROUPS = 4
D = 128
MESH = pl.DeviceIdType.MESH
F32 = jnp.float32
BF16 = jnp.bfloat16
NEG = -1e30
NEAR = (-2, -1, 0, 1, 2)
FAR = (-3, 3, 4)


def kernel(n_kv, n_seq, rows, q_hbm, k_hbm, v_hbm, docs_hbm, beta_hbm, gain_hbm, out_hbm,
           docs_ref, beta_ref, gain_ref, q_vm, k_vm, kv, docs, bias, top, total, acc, att, p_own, p_in, c_own, c_in, x_own, x_in, m_own, mem,
           in_sem, out_sem, ring_send, ring_recv, doc_send, doc_recv, p_send, p_recv, st_send, st_recv, mem_send, mem_recv):
    me = lax.axis_index("kv")
    seq = lax.axis_index("seq")
    core = lax.rem(seq, 2)
    other = seq + 1 - 2 * core
    chip = seq // 2
    half = n_kv // 2
    part = D // 2
    mine = 2 * lax.rem(me, GROUPS) + core
    odd_step = 4 * lax.rem(me, 2) - 2
    steps = (1, -1, odd_step, 0)

    def away(step):
        return lax.rem(me + step + n_kv, n_kv)

    def along(step):
        return lax.rem(seq + 2 * step + n_seq, n_seq)

    barrier = pltpu.get_barrier_semaphore()
    for d in range(1, n_kv):
        pl.semaphore_signal(barrier, inc=1, device_id={"kv": away(d)}, device_id_type=MESH)
        pl.semaphore_signal(barrier, inc=1, device_id={"kv": away(d), "seq": other}, device_id_type=MESH)
    for d in (other, along(1), along(2), along(-1), along(-2)):
        pl.semaphore_signal(barrier, inc=1, device_id={"seq": d}, device_id_type=MESH)

    def k_in(g):
        return pltpu.make_async_copy(k_hbm.at[:, pl.ds(g * D, D)], k_vm.at[g], in_sem.at[g])

    def v_in(g):
        return pltpu.make_async_copy(
            v_hbm.at[:, pl.ds(g * D, D)], kv.at[g, me, pl.ds(D, rows)], in_sem.at[GROUPS + g])

    def q_in(h):
        cols = pl.ds(pl.multiple_of(h * D, D), D)
        return pltpu.make_async_copy(q_hbm.at[:, cols], q_vm.at[h], in_sem.at[2 * GROUPS + h])

    smalls = [pltpu.make_async_copy(a, b, in_sem.at[2 * GROUPS + HEADS + n]) for n, (a, b) in enumerate(
        ((docs_hbm, docs_ref), (beta_hbm, beta_ref), (gain_hbm, gain_ref)))]
    smalls[0].start()
    for g in range(GROUPS):
        k_in(g).start()
    for g in range(GROUPS):
        v_in(g).start()
    smalls[1].start()
    smalls[2].start()
    for h in range(HEADS):
        q_in(h).start()
    smalls[0].wait()
    docs[core, me] = jnp.broadcast_to(docs_ref[...].astype(BF16), (16, rows))
    for j in range(half, n_kv):
        @pl.when(j > me)
        def _():
            for g in range(GROUPS):
                kv[g, j] = jnp.zeros((D + rows, D), BF16)
    for g in range(GROUPS):
        k_in(g).wait()
        kv[g, me, 0:D] = k_vm[g].T
    own_row = docs_ref[...].astype(F32)
    own_last = jnp.max(own_row, axis=1, keepdims=True)
    ending = jnp.where(own_row == own_last, 1.0, 0.0).astype(BF16)
    for g in range(GROUPS):
        v_in(g).wait()
        p = jnp.dot(kv[g, me, 0:D] * ending, kv[g, me, D:D + rows], preferred_element_type=F32)
        for n in range(D // part):
            p_own[g * (D // part) + n] = p[n * part:(n + 1) * part]
    pl.semaphore_wait(barrier, 2 * (n_kv - 1) + 5)

    def core_at(same):
        return (core, seq) if same else (1 - core, other)

    others = [(d, same) for d in range(n_kv) for same in (True, False) if d or not same]
    partners = [(n, same) for n in range(4) for same in (True, False) if n < 3 or not same]

    def doc_copy(d, same):
        c, s = core_at(same)
        ref = docs.at[core, me]
        return pltpu.make_async_remote_copy(
            src_ref=ref, dst_ref=ref, send_sem=doc_send.at[d, c], recv_sem=doc_recv.at[d, core],
            device_id={"kv": away(d), "seq": s}, device_id_type=MESH)

    def doc_arrival(d, same):
        c, s = core_at(same)
        ref = docs.at[c, away(-d)]
        return pltpu.make_async_remote_copy(
            src_ref=ref, dst_ref=ref, send_sem=doc_send.at[d, c], recv_sem=doc_recv.at[d, c],
            device_id={"kv": away(d), "seq": other}, device_id_type=MESH)

    def part_copy(n, same):
        c, s = core_at(same)
        to = away(steps[n])
        return pltpu.make_async_remote_copy(
            src_ref=p_own.at[2 * lax.rem(to, GROUPS) + c], dst_ref=p_in.at[n, core],
            send_sem=p_send.at[n, c], recv_sem=p_recv.at[n, core],
            device_id={"kv": to, "seq": s}, device_id_type=MESH)

    def part_arrival(n, same):
        c, s = core_at(same)
        return pltpu.make_async_remote_copy(
            src_ref=p_own.at[mine], dst_ref=p_in.at[n, c],
            send_sem=p_send.at[n, c], recv_sem=p_recv.at[n, c],
            device_id={"kv": me, "seq": other}, device_id_type=MESH)

    def span(h, onward):
        if h < half - 1:
            return pl.ds(0, D + rows)
        return pl.ds(0, D) if onward else pl.ds(D, rows)

    def ring(onward, g, h, ahead):
        blk = away(-h - ahead if onward else h + ahead)
        ref = kv.at[g, blk, span(h, onward)]
        t = 0 if onward else 1
        return pltpu.make_async_remote_copy(
            src_ref=ref, dst_ref=ref, send_sem=ring_send.at[t, g, h], recv_sem=ring_recv.at[t, g, h],
            device_id={"kv": away(1 if onward else -1)}, device_id_type=MESH)

    def sent(h, onward):
        return (me >= h) & (me < n_kv - 1) if onward else away(h) < half

    def arrives(h, onward):
        return me > h if onward else away(h + 1) < half

    def send(g, h):
        for onward in (True, False):
            @pl.when(sent(h, onward))
            def _():
                ring(onward, g, h, 0).start()

    def hop(g, h):
        for onward in (True, False):
            @pl.when(arrives(h, onward))
            def _():
                ring(onward, g, h, 1).wait_recv()
            if h + 1 < half:
                @pl.when(sent(h + 1, onward))
                def _():
                    ring(onward, g, h + 1, 0).start()

    def state_along(step):
        return pltpu.make_async_remote_copy(
            src_ref=c_own, dst_ref=c_in.at[step - 1], send_sem=st_send.at[step - 1], recv_sem=st_recv.at[step - 1],
            device_id={"seq": along(step)}, device_id_type=MESH)

    def state_across():
        return pltpu.make_async_remote_copy(
            src_ref=x_own, dst_ref=x_in, send_sem=st_send.at[2], recv_sem=st_recv.at[2],
            device_id={"kv": away(half)}, device_id_type=MESH)

    def memory_out(n, same):
        c, s = core_at(same)
        return pltpu.make_async_remote_copy(
            src_ref=m_own.at[c], dst_ref=mem.at[mine],
            send_sem=mem_send.at[n, c], recv_sem=mem_recv.at[n, core],
            device_id={"kv": away(steps[n]), "seq": s}, device_id_type=MESH)

    def memory_in(n, same):
        c, s = core_at(same)
        g = lax.rem(me + (GROUPS - 1, 1, 2, 0)[n], GROUPS)
        return pltpu.make_async_remote_copy(
            src_ref=m_own.at[c], dst_ref=mem.at[2 * g + c], send_sem=mem_send.at[n, c], recv_sem=mem_recv.at[n, c],
            device_id={"kv": me, "seq": other}, device_id_type=MESH)

    own_doc = jnp.broadcast_to(own_row, (rows, rows)).T

    def doc_row(j, c=None):
        return docs[core if c is None else c, j].astype(F32)[0:1]

    def ends():
        last = jnp.max(doc_row(n_kv - 1), axis=1, keepdims=True)
        first = jnp.min(doc_row(0), axis=1, keepdims=True)
        return first, last

    def masks():
        row = lax.broadcasted_iota(jnp.int32, (rows, rows), 0)
        lane = lax.broadcasted_iota(jnp.int32, (rows, rows), 1)
        for j in range(n_kv):
            allowed = (doc_row(j) == own_doc) & (j * rows + lane <= me * rows + row)
            bias[j] = jnp.where(allowed, 0.0, NEG)

    scale = math.log2(math.e) / math.sqrt(D)

    def mixing(h):
        return jax.nn.sigmoid(jnp.full((1, D), beta_ref[h], F32))

    def scores(i, offs):
        g = i // 2
        q2 = jnp.concatenate([q_vm[2 * i], q_vm[2 * i + 1]], axis=0)
        kt = jnp.concatenate([kv[g, away(o), 0:D] for o in offs], axis=1)
        b = jnp.concatenate([bias[away(o)] for o in offs], axis=1)
        s = jnp.dot(q2, kt, preferred_element_type=F32)
        return s + jnp.concatenate([b, b], axis=0)

    def weighted(i, offs, p):
        v = jnp.concatenate([kv[i // 2, away(o), D:D + rows] for o in offs], axis=0)
        return jnp.dot(p.astype(BF16), v, preferred_element_type=F32)

    def near(i):
        s = scores(i, NEAR)
        m = jnp.max(s, axis=-1, keepdims=True)
        p = jnp.exp2((s - m) * scale)
        top[i] = m
        total[i] = jnp.sum(p, axis=-1, keepdims=True)
        acc[i] = weighted(i, NEAR, p)

    def far(i):
        s = scores(i, FAR)
        old = top[i]
        m = jnp.maximum(old, jnp.max(s, axis=-1, keepdims=True))
        p = jnp.exp2((s - m) * scale)
        kept = jnp.exp2((old - m) * scale)
        norm = total[i] * kept + jnp.sum(p, axis=-1, keepdims=True)
        o = (acc[i] * kept + weighted(i, FAR, p)) / norm
        att[2 * i] = o[:rows] * (1.0 - mixing(2 * i))
        att[2 * i + 1] = o[rows:] * (1.0 - mixing(2 * i + 1))

    def settle(i):
        o = acc[i] / total[i]
        att[2 * i] = o[:rows] * (1.0 - mixing(2 * i))
        att[2 * i + 1] = o[rows:] * (1.0 - mixing(2 * i + 1))

    def rest(i):
        pl.when(me >= 3)(lambda: far(i))
        pl.when(me < 3)(lambda: settle(i))

    def some(f, start, stop):
        pl.loop(start, stop)(f)

    def edges(c):
        last = jnp.max(doc_row(n_kv - 1, c), axis=1, keepdims=True)
        first = jnp.min(doc_row(0, c), axis=1, keepdims=True)
        return first, last

    def tail_state():
        p_in[3, core] = p_own[mine]
        for n, same in partners:
            part_arrival(n, same).wait_recv()
        states = []
        for c in range(2):
            first, last = edges(c)

            def counted(n):
                here = jnp.max(doc_row(away(-steps[n]), c), axis=1, keepdims=True)
                return jnp.where(here == last, p_in[n, c], 0.0)

            states.append((sum(counted(n) for n in range(4)), first, last))
        (even, _, even_last), (odd, odd_first, odd_last) = states
        c_own[0:part] = odd + jnp.where(even_last == odd_last, even, 0.0)
        c_own[part:part + 8] = jnp.broadcast_to(odd_last, (8, D))
        state_along(1).start()
        state_along(2).start()
        x_own[1] = jnp.where(even_last == odd_first, even, 0.0)

    def part_memory():
        state_along(1).wait_recv()
        state_along(2).wait_recv()
        one, two = c_in[0], c_in[1]
        for c in range(2):
            first = edges(c)[0]
            m = jnp.where((one[part:part + 1] == first) & (chip >= 1), one[0:part], 0.0)
            m = m + jnp.where((two[part:part + 1] == first) & (chip >= 2), two[0:part], 0.0)
            x_own[c] = m + x_own[1] if c else m
        state_across().start()

    def own_memory():
        state_across().wait_recv()
        m_own[...] = x_own[...] + x_in[...]
        mem[mine] = x_own[core] + x_in[core]
        for n, same in partners:
            memory_out(n, same).start()

    def out_copy(h):
        cols = pl.ds(pl.multiple_of(h * D, D), D)
        return pltpu.make_async_copy(att.at[h], out_hbm.at[:, cols], out_sem.at[h])

    def recall(g):
        live = jnp.where(own_doc[:, 0:1] == ends()[0], 1.0, 0.0)
        state = jnp.concatenate([mem[g * (D // part) + n] for n in range(D // part)], axis=0)
        hi = state.astype(BF16)
        lo = (state - hi.astype(F32)).astype(BF16)
        both = jnp.concatenate([hi, lo], axis=1)
        q4 = jnp.concatenate([q_vm[4 * g + k] for k in range(4)], axis=0)
        r = jnp.dot(q4, both, preferred_element_type=F32)
        r = r[:, 0:D] + r[:, D:]
        for k in range(4):
            h = 4 * g + k
            rh = r[k * rows:(k + 1) * rows] * live
            mean = jnp.mean(rh * rh, axis=-1, keepdims=True)
            cols = pl.ds(pl.multiple_of(h * D, D), D)
            att[h] = att[h] + rh * lax.rsqrt(mean + 1e-6) * (gain_ref[:, cols] * mixing(h))
            out_copy(h).start()

    for d, same in others:
        doc_copy(d, same).start()
    for n, same in partners:
        part_copy(n, same).start()
    for g in range(GROUPS):
        send(g, 0)
    for d, same in others:
        doc_arrival(d, same).wait_recv()
    tail_state()
    hop(0, 0)
    masks()
    for h in range(HEADS):
        q_in(h).wait()
    smalls[1].wait()
    smalls[2].wait()
    hop(1, 0)
    hop(2, 0)
    hop(3, 0)
    part_memory()
    hop(0, 1)
    hop(1, 1)
    some(near, 0, 1)
    hop(2, 1)
    own_memory()
    some(near, 1, 3)
    hop(3, 1)
    some(near, 3, 4)
    hop(0, 2)
    some(near, 4, 5)
    hop(1, 2)
    some(near, 5, 6)
    hop(2, 2)
    some(near, 6, 7)
    hop(3, 2)
    some(near, 7, 8)
    for n, same in partners:
        memory_in(n, same).wait_recv()
    hop(0, 3)
    some(rest, 0, 2)
    some(recall, 0, 1)
    hop(1, 3)
    some(rest, 2, 4)
    some(recall, 1, 2)
    hop(2, 3)
    some(rest, 4, 6)
    some(recall, 2, 3)
    hop(3, 3)
    some(rest, 6, 8)
    some(recall, 3, 4)

    for h in range(half):
        for onward in (True, False):
            @pl.when(sent(h, onward))
            def _():
                for g in range(GROUPS):
                    ring(onward, g, h, 0).wait_send()
    for d, same in others:
        doc_copy(d, same).wait_send()
    for n, same in partners:
        part_copy(n, same).wait_send()
        memory_out(n, same).wait_send()
    state_along(1).wait_send()
    state_along(2).wait_send()
    state_across().wait_send()
    for h in range(HEADS):
        out_copy(h).wait()


def on_device(n_kv, n_seq, queries, keys, values, doc_ids, beta, lin_gain):
    rows = queries.shape[0]
    dma = pltpu.SemaphoreType.DMA
    part = D // 2
    return pl.pallas_call(
        functools.partial(kernel, n_kv, n_seq, rows),
        out_shape=jax.ShapeDtypeStruct((rows, HEADS * D), F32),
        in_specs=[pl.BlockSpec(memory_space=pltpu.HBM)] * 6,
        out_specs=pl.BlockSpec(memory_space=pl.ANY),
        scratch_shapes=[
            pltpu.VMEM((1, rows), jnp.int32),
            pltpu.SMEM((HEADS,), F32),
            pltpu.VMEM((1, HEADS * D), F32),
            pltpu.VMEM((HEADS, rows, D), BF16),
            pltpu.VMEM((GROUPS, rows, D), BF16),
            pltpu.VMEM((GROUPS, n_kv, D + rows, D), BF16),
            pltpu.VMEM((2, n_kv, 16, rows), BF16),
            pltpu.VMEM((n_kv, rows, rows), F32),
            pltpu.VMEM((HEADS // 2, 2 * rows, 1), F32),
            pltpu.VMEM((HEADS // 2, 2 * rows, 1), F32),
            pltpu.VMEM((HEADS // 2, 2 * rows, D), F32),
            pltpu.VMEM((HEADS, rows, D), F32),
            pltpu.VMEM((2 * GROUPS, part, D), F32),
            pltpu.VMEM((4, 2, part, D), F32),
            pltpu.VMEM((part + 8, D), F32),
            pltpu.VMEM((2, part + 8, D), F32),
            pltpu.VMEM((2, part, D), F32),
            pltpu.VMEM((2, part, D), F32),
            pltpu.VMEM((2, part, D), F32),
            pltpu.VMEM((2 * GROUPS, part, D), F32),
            dma((2 * GROUPS + HEADS + 3,)),
            dma((HEADS,)),
            dma((2, GROUPS, n_kv // 2)),
            dma((2, GROUPS, n_kv // 2)),
            dma((n_kv, 2)),
            dma((n_kv, 2)),
            dma((4, 2)),
            dma((4, 2)),
            dma((3,)),
            dma((3,)),
            dma((4, 2)),
            dma((4, 2)),
        ],
        compiler_params=pltpu.CompilerParams(
            collective_id=0, has_side_effects=True, vmem_limit_bytes=60 * 1024 * 1024),
    )(queries, keys, values, doc_ids.reshape(1, rows), beta, lin_gain.reshape(1, HEADS * D))


def solution(mesh):
    split = P(("dp", "seq", "kv"))
    rows = P(("dp", "seq", "kv"), None)
    return jax.shard_map(
        functools.partial(on_device, mesh.shape["kv"], mesh.shape["seq"]),
        mesh=mesh, in_specs=(rows, rows, rows, split, P(), P()), out_specs=rows, check_vma=False)
```

```python
import functools
import math

import jax
import jax.numpy as jnp
from jax import lax
from jax.experimental import pallas as pl
from jax.experimental.pallas import tpu as pltpu
from jax.sharding import PartitionSpec as P

HEADS = 16
GROUPS = 4
D = 128
MESH = pl.DeviceIdType.MESH
F32 = jnp.float32
BF16 = jnp.bfloat16
NEG = -1e30
NEAR = (-2, -1, 0, 1, 2)
BACK = (-2, -1, 0)
FAR = (-3, 3, 4)


def kernel(n_kv, n_seq, rows, q_hbm, k_hbm, v_hbm, docs_hbm, beta_hbm, gain_hbm, out_hbm,
           docs_ref, beta_ref, gain_ref, q_vm, k_vm, kv, docs, bias, top, total, acc, att, p_own, p_in, c_own, c_in, x_own, x_in, m_own, mem,
           in_sem, out_sem, ring_send, ring_recv, doc_send, doc_recv, p_send, p_recv, st_send, st_recv, mem_send, mem_recv):
    me = lax.axis_index("kv")
    seq = lax.axis_index("seq")
    core = lax.rem(seq, 2)
    other = seq + 1 - 2 * core
    chip = seq // 2
    half = n_kv // 2
    part = D // 2
    mine = 2 * lax.rem(me, GROUPS) + core
    odd_step = 4 * lax.rem(me, 2) - 2
    steps = (1, -1, odd_step, 0)

    def away(step):
        return lax.rem(me + step + n_kv, n_kv)

    def along(step):
        return lax.rem(seq + 2 * step + n_seq, n_seq)

    barrier = pltpu.get_barrier_semaphore()
    for d in range(1, n_kv):
        pl.semaphore_signal(barrier, inc=1, device_id={"kv": away(d)}, device_id_type=MESH)
        pl.semaphore_signal(barrier, inc=1, device_id={"kv": away(d), "seq": other}, device_id_type=MESH)
    for d in (other, along(1), along(2), along(-1), along(-2)):
        pl.semaphore_signal(barrier, inc=1, device_id={"seq": d}, device_id_type=MESH)

    def k_in(g):
        return pltpu.make_async_copy(k_hbm.at[:, pl.ds(g * D, D)], k_vm.at[g], in_sem.at[g])

    def v_in(g):
        return pltpu.make_async_copy(
            v_hbm.at[:, pl.ds(g * D, D)], kv.at[g, me, pl.ds(D, rows)], in_sem.at[GROUPS + g])

    def q_in(h):
        cols = pl.ds(pl.multiple_of(h * D, D), D)
        return pltpu.make_async_copy(q_hbm.at[:, cols], q_vm.at[h], in_sem.at[2 * GROUPS + h])

    smalls = [pltpu.make_async_copy(a, b, in_sem.at[2 * GROUPS + HEADS + n]) for n, (a, b) in enumerate(
        ((docs_hbm, docs_ref), (beta_hbm, beta_ref), (gain_hbm, gain_ref)))]
    smalls[0].start()
    for g in range(GROUPS):
        k_in(g).start()
    for g in range(GROUPS):
        v_in(g).start()
    smalls[1].start()
    smalls[2].start()
    for h in range(HEADS):
        q_in(h).start()
    smalls[0].wait()
    docs[core, me] = jnp.broadcast_to(docs_ref[...].astype(BF16), (16, rows))
    for j in range(half, n_kv):
        @pl.when(j > me)
        def _():
            for g in range(GROUPS):
                kv[g, j] = jnp.zeros((D + rows, D), BF16)
    for g in range(GROUPS):
        k_in(g).wait()
        kv[g, me, 0:D] = k_vm[g].T
    own_row = docs_ref[...].astype(F32)
    own_last = jnp.max(own_row, axis=1, keepdims=True)
    ending = jnp.where(own_row == own_last, 1.0, 0.0).astype(BF16)
    for g in range(GROUPS):
        v_in(g).wait()
        p = jnp.dot(kv[g, me, 0:D] * ending, kv[g, me, D:D + rows], preferred_element_type=F32)
        for n in range(D // part):
            p_own[g * (D // part) + n] = p[n * part:(n + 1) * part]
    pl.semaphore_wait(barrier, 2 * (n_kv - 1) + 5)

    def core_at(same):
        return (core, seq) if same else (1 - core, other)

    others = [(d, same) for d in range(n_kv) for same in (True, False) if d or not same]
    partners = [(n, same) for n in range(4) for same in (True, False) if n < 3 or not same]

    def doc_copy(d, same):
        c, s = core_at(same)
        ref = docs.at[core, me]
        return pltpu.make_async_remote_copy(
            src_ref=ref, dst_ref=ref, send_sem=doc_send.at[d, c], recv_sem=doc_recv.at[d, core],
            device_id={"kv": away(d), "seq": s}, device_id_type=MESH)

    def doc_arrival(d, same):
        c, s = core_at(same)
        ref = docs.at[c, away(-d)]
        return pltpu.make_async_remote_copy(
            src_ref=ref, dst_ref=ref, send_sem=doc_send.at[d, c], recv_sem=doc_recv.at[d, c],
            device_id={"kv": away(d), "seq": other}, device_id_type=MESH)

    def part_copy(n, same):
        c, s = core_at(same)
        to = away(steps[n])
        return pltpu.make_async_remote_copy(
            src_ref=p_own.at[2 * lax.rem(to, GROUPS) + c], dst_ref=p_in.at[n, core],
            send_sem=p_send.at[n, c], recv_sem=p_recv.at[n, core],
            device_id={"kv": to, "seq": s}, device_id_type=MESH)

    def part_arrival(n, same):
        c, s = core_at(same)
        return pltpu.make_async_remote_copy(
            src_ref=p_own.at[mine], dst_ref=p_in.at[n, c],
            send_sem=p_send.at[n, c], recv_sem=p_recv.at[n, c],
            device_id={"kv": me, "seq": other}, device_id_type=MESH)

    def span(h, onward, whole):
        if h < half - 1 and whole:
            return pl.ds(0, D + rows)
        return pl.ds(0, D) if onward else pl.ds(D, rows)

    def ring(onward, g, h, ahead, whole=True):
        blk = away(-h - ahead if onward else h + ahead)
        ref = kv.at[g, blk, span(h, onward, whole)]
        t = 0 if onward else 1
        return pltpu.make_async_remote_copy(
            src_ref=ref, dst_ref=ref, send_sem=ring_send.at[t, g, h], recv_sem=ring_recv.at[t, g, h],
            device_id={"kv": away(1 if onward else -1)}, device_id_type=MESH)

    def legs(h, ahead):
        right_on = (me >= h) & (me < n_kv - 1) if ahead == 0 else me > h
        blk = away(h + ahead)
        if h == half - 1:
            return ((True, right_on, True), (False, blk < half, True))
        return ((True, right_on, True), (False, blk < half - 1, True), (False, blk == half - 1, False))

    def send(g, h):
        for onward, on, whole in legs(h, 0):
            @pl.when(on)
            def _():
                ring(onward, g, h, 0, whole).start()

    def hop(g, h):
        for onward, on, whole in legs(h, 1):
            @pl.when(on)
            def _():
                ring(onward, g, h, 1, whole).wait_recv()
        if h + 1 < half:
            send(g, h + 1)

    def state_along(step):
        return pltpu.make_async_remote_copy(
            src_ref=c_own, dst_ref=c_in.at[step - 1], send_sem=st_send.at[step - 1], recv_sem=st_recv.at[step - 1],
            device_id={"seq": along(step)}, device_id_type=MESH)

    def state_across():
        return pltpu.make_async_remote_copy(
            src_ref=x_own, dst_ref=x_in, send_sem=st_send.at[2], recv_sem=st_recv.at[2],
            device_id={"kv": away(half)}, device_id_type=MESH)

    def memory_out(n, same):
        c, s = core_at(same)
        return pltpu.make_async_remote_copy(
            src_ref=m_own.at[c], dst_ref=mem.at[mine],
            send_sem=mem_send.at[n, c], recv_sem=mem_recv.at[n, core],
            device_id={"kv": away(steps[n]), "seq": s}, device_id_type=MESH)

    def memory_in(n, same):
        c, s = core_at(same)
        g = lax.rem(me + (GROUPS - 1, 1, 2, 0)[n], GROUPS)
        return pltpu.make_async_remote_copy(
            src_ref=m_own.at[c], dst_ref=mem.at[2 * g + c], send_sem=mem_send.at[n, c], recv_sem=mem_recv.at[n, c],
            device_id={"kv": me, "seq": other}, device_id_type=MESH)

    own_doc = jnp.broadcast_to(own_row, (rows, rows)).T

    def doc_row(j, c=None):
        return docs[core if c is None else c, j].astype(F32)[0:1]

    def ends():
        last = jnp.max(doc_row(n_kv - 1), axis=1, keepdims=True)
        first = jnp.min(doc_row(0), axis=1, keepdims=True)
        return first, last

    def masks():
        row = lax.broadcasted_iota(jnp.int32, (rows, rows), 0)
        lane = lax.broadcasted_iota(jnp.int32, (rows, rows), 1)
        for j in range(n_kv):
            allowed = (doc_row(j) == own_doc) & (j * rows + lane <= me * rows + row)
            bias[j] = jnp.where(allowed, 0.0, NEG)

    scale = math.log2(math.e) / math.sqrt(D)

    def mixing(h):
        return jax.nn.sigmoid(jnp.full((1, D), beta_ref[h], F32))

    def scores(i, offs):
        g = i // 2
        q2 = jnp.concatenate([q_vm[2 * i], q_vm[2 * i + 1]], axis=0)
        kt = jnp.concatenate([kv[g, away(o), 0:D] for o in offs], axis=1)
        b = jnp.concatenate([bias[away(o)] for o in offs], axis=1)
        s = jnp.dot(q2, kt, preferred_element_type=F32)
        return s + jnp.concatenate([b, b], axis=0)

    def weighted(i, offs, p):
        v = jnp.concatenate([kv[i // 2, away(o), D:D + rows] for o in offs], axis=0)
        return jnp.dot(p.astype(BF16), v, preferred_element_type=F32)

    def first_pass(i, offs):
        s = scores(i, offs)
        m = jnp.max(s, axis=-1, keepdims=True)
        p = jnp.exp2((s - m) * scale)
        top[i] = m
        total[i] = jnp.sum(p, axis=-1, keepdims=True)
        acc[i] = weighted(i, offs, p)

    def near(i):
        pl.when(me < n_kv - 2)(lambda: first_pass(i, BACK))
        pl.when(me >= n_kv - 2)(lambda: first_pass(i, NEAR))

    def far(i, offs):
        s = scores(i, offs)
        old = top[i]
        m = jnp.maximum(old, jnp.max(s, axis=-1, keepdims=True))
        p = jnp.exp2((s - m) * scale)
        kept = jnp.exp2((old - m) * scale)
        norm = total[i] * kept + jnp.sum(p, axis=-1, keepdims=True)
        o = (acc[i] * kept + weighted(i, offs, p)) / norm
        att[2 * i] = o[:rows] * (1.0 - mixing(2 * i))
        att[2 * i + 1] = o[rows:] * (1.0 - mixing(2 * i + 1))

    def settle(i):
        o = acc[i] / total[i]
        att[2 * i] = o[:rows] * (1.0 - mixing(2 * i))
        att[2 * i + 1] = o[rows:] * (1.0 - mixing(2 * i + 1))

    def some(f, start, stop):
        pl.loop(start, stop)(f)

    def edges(c):
        last = jnp.max(doc_row(n_kv - 1, c), axis=1, keepdims=True)
        first = jnp.min(doc_row(0, c), axis=1, keepdims=True)
        return first, last

    def tail_state():
        p_in[3, core] = p_own[mine]
        for n, same in partners:
            part_arrival(n, same).wait_recv()
        states = []
        for c in range(2):
            first, last = edges(c)

            def counted(n):
                here = jnp.max(doc_row(away(-steps[n]), c), axis=1, keepdims=True)
                return jnp.where(here == last, p_in[n, c], 0.0)

            states.append((sum(counted(n) for n in range(4)), first, last))
        (even, _, even_last), (odd, odd_first, odd_last) = states
        c_own[0:part] = odd + jnp.where(even_last == odd_last, even, 0.0)
        c_own[part:part + 8] = jnp.broadcast_to(odd_last, (8, D))
        state_along(1).start()
        state_along(2).start()
        x_own[1] = jnp.where(even_last == odd_first, even, 0.0)

    def part_memory():
        state_along(1).wait_recv()
        state_along(2).wait_recv()
        one, two = c_in[0], c_in[1]
        for c in range(2):
            first = edges(c)[0]
            m = jnp.where((one[part:part + 1] == first) & (chip >= 1), one[0:part], 0.0)
            m = m + jnp.where((two[part:part + 1] == first) & (chip >= 2), two[0:part], 0.0)
            x_own[c] = m + x_own[1] if c else m
        state_across().start()

    def own_memory():
        state_across().wait_recv()
        m_own[...] = x_own[...] + x_in[...]
        mem[mine] = x_own[core] + x_in[core]
        for n, same in partners:
            memory_out(n, same).start()

    def out_copy(h):
        cols = pl.ds(pl.multiple_of(h * D, D), D)
        return pltpu.make_async_copy(att.at[h], out_hbm.at[:, cols], out_sem.at[h])

    def recall(g):
        live = jnp.where(own_doc[:, 0:1] == ends()[0], 1.0, 0.0)
        state = jnp.concatenate([mem[g * (D // part) + n] for n in range(D // part)], axis=0)
        hi = state.astype(BF16)
        lo = (state - hi.astype(F32)).astype(BF16)
        both = jnp.concatenate([hi, lo], axis=1)
        q4 = jnp.concatenate([q_vm[4 * g + k] for k in range(4)], axis=0)
        r = jnp.dot(q4, both, preferred_element_type=F32)
        r = r[:, 0:D] + r[:, D:]
        for k in range(4):
            h = 4 * g + k
            rh = r[k * rows:(k + 1) * rows] * live
            mean = jnp.mean(rh * rh, axis=-1, keepdims=True)
            cols = pl.ds(pl.multiple_of(h * D, D), D)
            att[h] = att[h] + rh * lax.rsqrt(mean + 1e-6) * (gain_ref[:, cols] * mixing(h))
            out_copy(h).start()

    for d, same in others:
        doc_copy(d, same).start()
    for n, same in partners:
        part_copy(n, same).start()
    for g in range(GROUPS):
        send(g, 0)
    for d, same in others:
        doc_arrival(d, same).wait_recv()
    tail_state()
    hop(0, 0)
    masks()
    for h in range(HEADS):
        q_in(h).wait()
    smalls[1].wait()
    smalls[2].wait()
    hop(1, 0)
    hop(2, 0)
    hop(3, 0)
    part_memory()
    hop(0, 1)
    hop(1, 1)
    hop(2, 1)
    hop(3, 1)

    @pl.loop(0, HEADS // 2)
    def _(i):
        near(i)

        @pl.when(i == 0)
        def _():
            own_memory()
            hop(0, 2)

        @pl.when(i == 2)
        def _():
            hop(1, 2)

        @pl.when(i == 4)
        def _():
            hop(2, 2)

        @pl.when(i == 6)
        def _():
            hop(3, 2)

    @pl.when(me < half)
    def _():
        @pl.loop(0, HEADS // 2)
        def _(i):
            pl.when(me == half - 1)(lambda: far(i, FAR[:1]))
            pl.when(me < half - 1)(lambda: settle(i))

        for n, same in partners:
            memory_in(n, same).wait_recv()
        some(recall, 0, GROUPS)

    @pl.when(me >= half)
    def _():
        @pl.loop(0, GROUPS)
        def _(g):
            for ahead in range(GROUPS):
                @pl.when(g == ahead)
                def _():
                    hop(ahead, half - 1)

            @pl.loop(2 * g, 2 * g + 2)
            def _(i):
                far(i, FAR)

            @pl.when(g == 0)
            def _():
                for n, same in partners:
                    memory_in(n, same).wait_recv()

            recall(g)

    for h in range(half):
        for onward, on, whole in legs(h, 0):
            @pl.when(on)
            def _():
                for g in range(GROUPS):
                    ring(onward, g, h, 0, whole).wait_send()
    for d, same in others:
        doc_copy(d, same).wait_send()
    for n, same in partners:
        part_copy(n, same).wait_send()
        memory_out(n, same).wait_send()
    state_along(1).wait_send()
    state_along(2).wait_send()
    state_across().wait_send()
    for h in range(HEADS):
        out_copy(h).wait()


def on_device(n_kv, n_seq, queries, keys, values, doc_ids, beta, lin_gain):
    rows = queries.shape[0]
    dma = pltpu.SemaphoreType.DMA
    part = D // 2
    return pl.pallas_call(
        functools.partial(kernel, n_kv, n_seq, rows),
        out_shape=jax.ShapeDtypeStruct((rows, HEADS * D), F32),
        in_specs=[pl.BlockSpec(memory_space=pltpu.HBM)] * 6,
        out_specs=pl.BlockSpec(memory_space=pl.ANY),
        scratch_shapes=[
            pltpu.VMEM((1, rows), jnp.int32),
            pltpu.SMEM((HEADS,), F32),
            pltpu.VMEM((1, HEADS * D), F32),
            pltpu.VMEM((HEADS, rows, D), BF16),
            pltpu.VMEM((GROUPS, rows, D), BF16),
            pltpu.VMEM((GROUPS, n_kv, D + rows, D), BF16),
            pltpu.VMEM((2, n_kv, 16, rows), BF16),
            pltpu.VMEM((n_kv, rows, rows), F32),
            pltpu.VMEM((HEADS // 2, 2 * rows, 1), F32),
            pltpu.VMEM((HEADS // 2, 2 * rows, 1), F32),
            pltpu.VMEM((HEADS // 2, 2 * rows, D), F32),
            pltpu.VMEM((HEADS, rows, D), F32),
            pltpu.VMEM((2 * GROUPS, part, D), F32),
            pltpu.VMEM((4, 2, part, D), F32),
            pltpu.VMEM((part + 8, D), F32),
            pltpu.VMEM((2, part + 8, D), F32),
            pltpu.VMEM((2, part, D), F32),
            pltpu.VMEM((2, part, D), F32),
            pltpu.VMEM((2, part, D), F32),
            pltpu.VMEM((2 * GROUPS, part, D), F32),
            dma((2 * GROUPS + HEADS + 3,)),
            dma((HEADS,)),
            dma((2, GROUPS, n_kv // 2)),
            dma((2, GROUPS, n_kv // 2)),
            dma((n_kv, 2)),
            dma((n_kv, 2)),
            dma((4, 2)),
            dma((4, 2)),
            dma((3,)),
            dma((3,)),
            dma((4, 2)),
            dma((4, 2)),
        ],
        compiler_params=pltpu.CompilerParams(
            collective_id=0, has_side_effects=True, vmem_limit_bytes=60 * 1024 * 1024),
    )(queries, keys, values, doc_ids.reshape(1, rows), beta, lin_gain.reshape(1, HEADS * D))


def solution(mesh):
    split = P(("dp", "seq", "kv"))
    rows = P(("dp", "seq", "kv"), None)
    return jax.shard_map(
        functools.partial(on_device, mesh.shape["kv"], mesh.shape["seq"]),
        mesh=mesh, in_specs=(rows, rows, rows, split, P(), P()), out_specs=rows, check_vma=False)
```

```python
import functools
import math

import jax
import jax.numpy as jnp
from jax import lax
from jax.experimental import pallas as pl
from jax.experimental.pallas import tpu as pltpu
from jax.sharding import PartitionSpec as P

HEADS = 16
GROUPS = 4
D = 128
MESH = pl.DeviceIdType.MESH
F32 = jnp.float32
BF16 = jnp.bfloat16
NEG = -1e30
NEAR = (-2, -1, 0, 1, 2)
BACK = (-2, -1, 0)
FAR = (-3, 3, 4)


def kernel(n_kv, n_seq, rows, q_hbm, k_hbm, v_hbm, docs_hbm, beta_hbm, gain_hbm, out_hbm,
           docs_ref, beta_ref, gain_ref, q_vm, k_vm, kv, docs, bias, top, total, acc, att, p_own, p_in, c_own, c_in, x_own, x_in, m_own, mem,
           in_sem, out_sem, ring_send, ring_recv, doc_send, doc_recv, p_send, p_recv, st_send, st_recv, mem_send, mem_recv):
    me = lax.axis_index("kv")
    seq = lax.axis_index("seq")
    core = lax.rem(seq, 2)
    other = seq + 1 - 2 * core
    chip = seq // 2
    half = n_kv // 2
    part = D // 2
    mine = 2 * lax.rem(me, GROUPS) + core
    odd_step = 4 * lax.rem(me, 2) - 2
    steps = (1, -1, odd_step, 0)

    def away(step):
        return lax.rem(me + step + n_kv, n_kv)

    def along(step):
        return lax.rem(seq + 2 * step + n_seq, n_seq)

    barrier = pltpu.get_barrier_semaphore()
    for d in range(1, n_kv):
        pl.semaphore_signal(barrier, inc=1, device_id={"kv": away(d)}, device_id_type=MESH)
    for d in (1, 2, -1, -2):
        pl.semaphore_signal(barrier, inc=1, device_id={"kv": away(d), "seq": other}, device_id_type=MESH)
    for d in (other, along(1), along(2), along(-1), along(-2)):
        pl.semaphore_signal(barrier, inc=1, device_id={"seq": d}, device_id_type=MESH)

    def k_in(g):
        return pltpu.make_async_copy(k_hbm.at[:, pl.ds(g * D, D)], k_vm.at[g], in_sem.at[g])

    def v_in(g):
        return pltpu.make_async_copy(
            v_hbm.at[:, pl.ds(g * D, D)], kv.at[g, me, pl.ds(D, rows)], in_sem.at[GROUPS + g])

    def q_in(h):
        cols = pl.ds(pl.multiple_of(h * D, D), D)
        return pltpu.make_async_copy(q_hbm.at[:, cols], q_vm.at[h], in_sem.at[2 * GROUPS + h])

    smalls = [pltpu.make_async_copy(a, b, in_sem.at[2 * GROUPS + HEADS + n]) for n, (a, b) in enumerate(
        ((docs_hbm, docs_ref), (beta_hbm, beta_ref), (gain_hbm, gain_ref)))]
    smalls[0].start()
    for g in range(GROUPS):
        k_in(g).start()
    for g in range(GROUPS):
        v_in(g).start()
    smalls[0].wait()
    docs[core, me] = jnp.broadcast_to(docs_ref[...].astype(BF16), (16, rows))
    for j in range(half, n_kv):
        @pl.when(j > me)
        def _():
            for g in range(GROUPS):
                kv[g, j] = jnp.zeros((D + rows, D), BF16)
    for g in range(GROUPS):
        k_in(g).wait()
        kv[g, me, 0:D] = k_vm[g].T
    own_row = docs_ref[...].astype(F32)
    own_last = jnp.max(own_row, axis=1, keepdims=True)
    ending = jnp.where(own_row == own_last, 1.0, 0.0).astype(BF16)
    for g in range(GROUPS):
        v_in(g).wait()
        p = jnp.dot(kv[g, me, 0:D] * ending, kv[g, me, D:D + rows], preferred_element_type=F32)
        for n in range(D // part):
            p_own[g * (D // part) + n] = p[n * part:(n + 1) * part]
    pl.semaphore_wait(barrier, n_kv - 1 + 9)

    def core_at(same):
        return (core, seq) if same else (1 - core, other)

    others = [(d, same) for d in range(n_kv) for same in (True, False) if d or not same]
    partners = [(n, same) for n in range(4) for same in (True, False) if n < 3 or not same]

    def doc_copy(d):
        ref = docs.at[core, me]
        return pltpu.make_async_remote_copy(
            src_ref=ref, dst_ref=ref, send_sem=doc_send.at[d], recv_sem=doc_recv.at[d],
            device_id={"kv": away(d)}, device_id_type=MESH)

    def doc_arrival(d):
        ref = docs.at[core, away(-d)]
        return pltpu.make_async_remote_copy(
            src_ref=ref, dst_ref=ref, send_sem=doc_send.at[d], recv_sem=doc_recv.at[d],
            device_id={"kv": away(d)}, device_id_type=MESH)

    def doc_exchange(c):
        ref = docs.at[c]
        return pltpu.make_async_remote_copy(
            src_ref=ref, dst_ref=ref, send_sem=doc_send.at[0], recv_sem=doc_recv.at[0],
            device_id={"seq": other}, device_id_type=MESH)

    def part_copy(n, same):
        c, s = core_at(same)
        to = away(steps[n])
        return pltpu.make_async_remote_copy(
            src_ref=p_own.at[2 * lax.rem(to, GROUPS) + c], dst_ref=p_in.at[n, core],
            send_sem=p_send.at[n, c], recv_sem=p_recv.at[n, core],
            device_id={"kv": to, "seq": s}, device_id_type=MESH)

    def part_arrival(n, same):
        c, s = core_at(same)
        return pltpu.make_async_remote_copy(
            src_ref=p_own.at[mine], dst_ref=p_in.at[n, c],
            send_sem=p_send.at[n, c], recv_sem=p_recv.at[n, c],
            device_id={"kv": me, "seq": other}, device_id_type=MESH)

    def span(h, onward, whole):
        if h < half - 1 and whole:
            return pl.ds(0, D + rows)
        return pl.ds(0, D) if onward else pl.ds(D, rows)

    def ring(onward, g, h, ahead, whole=True):
        blk = away(-h - ahead if onward else h + ahead)
        ref = kv.at[g, blk, span(h, onward, whole)]
        t = 0 if onward else 1
        return pltpu.make_async_remote_copy(
            src_ref=ref, dst_ref=ref, send_sem=ring_send.at[t, g, h], recv_sem=ring_recv.at[t, g, h],
            device_id={"kv": away(1 if onward else -1)}, device_id_type=MESH)

    def legs(h, ahead):
        right_on = (me >= h) & (me < n_kv - 1) if ahead == 0 else me > h
        blk = away(h + ahead)
        if h == half - 1:
            return ((True, right_on, True), (False, blk < half, True))
        return ((True, right_on, True), (False, blk < half - 1, True), (False, blk == half - 1, False))

    def send(g, h):
        for onward, on, whole in legs(h, 0):
            @pl.when(on)
            def _():
                ring(onward, g, h, 0, whole).start()

    def hop(g, h):
        for onward, on, whole in legs(h, 1):
            @pl.when(on)
            def _():
                ring(onward, g, h, 1, whole).wait_recv()
        if h + 1 < half:
            send(g, h + 1)

    def state_along(step):
        return pltpu.make_async_remote_copy(
            src_ref=c_own, dst_ref=c_in.at[step - 1], send_sem=st_send.at[step - 1], recv_sem=st_recv.at[step - 1],
            device_id={"seq": along(step)}, device_id_type=MESH)

    def state_across():
        return pltpu.make_async_remote_copy(
            src_ref=x_own, dst_ref=x_in, send_sem=st_send.at[2], recv_sem=st_recv.at[2],
            device_id={"kv": away(half)}, device_id_type=MESH)

    def memory_out(n, same):
        c, s = core_at(same)
        return pltpu.make_async_remote_copy(
            src_ref=m_own.at[c], dst_ref=mem.at[mine],
            send_sem=mem_send.at[n, c], recv_sem=mem_recv.at[n, core],
            device_id={"kv": away(steps[n]), "seq": s}, device_id_type=MESH)

    def memory_in(n, same):
        c, s = core_at(same)
        g = lax.rem(me + (GROUPS - 1, 1, 2, 0)[n], GROUPS)
        return pltpu.make_async_remote_copy(
            src_ref=m_own.at[c], dst_ref=mem.at[2 * g + c], send_sem=mem_send.at[n, c], recv_sem=mem_recv.at[n, c],
            device_id={"kv": me, "seq": other}, device_id_type=MESH)

    own_doc = jnp.broadcast_to(own_row, (rows, rows)).T

    def doc_row(j, c=None):
        return docs[core if c is None else c, j].astype(F32)[0:1]

    def ends():
        last = jnp.max(doc_row(n_kv - 1), axis=1, keepdims=True)
        first = jnp.min(doc_row(0), axis=1, keepdims=True)
        return first, last

    def masks():
        row = lax.broadcasted_iota(jnp.int32, (rows, rows), 0)
        lane = lax.broadcasted_iota(jnp.int32, (rows, rows), 1)
        for j in range(n_kv):
            allowed = (doc_row(j) == own_doc) & (j * rows + lane <= me * rows + row)
            bias[j] = jnp.where(allowed, 0.0, NEG)

    scale = math.log2(math.e) / math.sqrt(D)

    def mixing(h):
        return jax.nn.sigmoid(jnp.full((1, D), beta_ref[h], F32))

    def scores(i, offs):
        g = i // 2
        q2 = jnp.concatenate([q_vm[2 * i], q_vm[2 * i + 1]], axis=0)
        kt = jnp.concatenate([kv[g, away(o), 0:D] for o in offs], axis=1)
        b = jnp.concatenate([bias[away(o)] for o in offs], axis=1)
        s = jnp.dot(q2, kt, preferred_element_type=F32)
        return s + jnp.concatenate([b, b], axis=0)

    def weighted(i, offs, p):
        v = jnp.concatenate([kv[i // 2, away(o), D:D + rows] for o in offs], axis=0)
        return jnp.dot(p.astype(BF16), v, preferred_element_type=F32)

    def first_pass(i, offs):
        s = scores(i, offs)
        m = jnp.max(s, axis=-1, keepdims=True)
        p = jnp.exp2((s - m) * scale)
        top[i] = m
        total[i] = jnp.sum(p, axis=-1, keepdims=True)
        acc[i] = weighted(i, offs, p)

    def near(i):
        pl.when(me < n_kv - 2)(lambda: first_pass(i, BACK))
        pl.when(me >= n_kv - 2)(lambda: first_pass(i, NEAR))

    def far(i, offs):
        s = scores(i, offs)
        old = top[i]
        m = jnp.maximum(old, jnp.max(s, axis=-1, keepdims=True))
        p = jnp.exp2((s - m) * scale)
        kept = jnp.exp2((old - m) * scale)
        norm = total[i] * kept + jnp.sum(p, axis=-1, keepdims=True)
        o = (acc[i] * kept + weighted(i, offs, p)) / norm
        att[2 * i] = o[:rows] * (1.0 - mixing(2 * i))
        att[2 * i + 1] = o[rows:] * (1.0 - mixing(2 * i + 1))

    def settle(i):
        o = acc[i] / total[i]
        att[2 * i] = o[:rows] * (1.0 - mixing(2 * i))
        att[2 * i + 1] = o[rows:] * (1.0 - mixing(2 * i + 1))

    def some(f, start, stop):
        pl.loop(start, stop)(f)

    def edges(c):
        last = jnp.max(doc_row(n_kv - 1, c), axis=1, keepdims=True)
        first = jnp.min(doc_row(0, c), axis=1, keepdims=True)
        return first, last

    def tail_state():
        p_in[3, core] = p_own[mine]
        for n, same in partners:
            part_arrival(n, same).wait_recv()
        states = []
        for c in range(2):
            first, last = edges(c)

            def counted(n):
                here = jnp.max(doc_row(away(-steps[n]), c), axis=1, keepdims=True)
                return jnp.where(here == last, p_in[n, c], 0.0)

            states.append((sum(counted(n) for n in range(4)), first, last))
        (even, _, even_last), (odd, odd_first, odd_last) = states
        c_own[0:part] = odd + jnp.where(even_last == odd_last, even, 0.0)
        c_own[part:part + 8] = jnp.broadcast_to(odd_last, (8, D))
        state_along(1).start()
        state_along(2).start()
        x_own[1] = jnp.where(even_last == odd_first, even, 0.0)

    def part_memory():
        state_along(1).wait_recv()
        state_along(2).wait_recv()
        one, two = c_in[0], c_in[1]
        for c in range(2):
            first = edges(c)[0]
            m = jnp.where((one[part:part + 1] == first) & (chip >= 1), one[0:part], 0.0)
            m = m + jnp.where((two[part:part + 1] == first) & (chip >= 2), two[0:part], 0.0)
            x_own[c] = m + x_own[1] if c else m
        state_across().start()

    def own_memory():
        state_across().wait_recv()
        m_own[...] = x_own[...] + x_in[...]
        mem[mine] = x_own[core] + x_in[core]
        for n, same in partners:
            memory_out(n, same).start()

    def out_copy(h):
        cols = pl.ds(pl.multiple_of(h * D, D), D)
        return pltpu.make_async_copy(att.at[h], out_hbm.at[:, cols], out_sem.at[h])

    def recall(g):
        live = jnp.where(own_doc[:, 0:1] == ends()[0], 1.0, 0.0)
        state = jnp.concatenate([mem[g * (D // part) + n] for n in range(D // part)], axis=0)
        hi = state.astype(BF16)
        lo = (state - hi.astype(F32)).astype(BF16)
        both = jnp.concatenate([hi, lo], axis=1)
        q4 = jnp.concatenate([q_vm[4 * g + k] for k in range(4)], axis=0)
        r = jnp.dot(q4, both, preferred_element_type=F32)
        r = r[:, 0:D] + r[:, D:]
        for k in range(4):
            h = 4 * g + k
            rh = r[k * rows:(k + 1) * rows] * live
            mean = jnp.mean(rh * rh, axis=-1, keepdims=True)
            cols = pl.ds(pl.multiple_of(h * D, D), D)
            att[h] = att[h] + rh * lax.rsqrt(mean + 1e-6) * (gain_ref[:, cols] * mixing(h))
            out_copy(h).start()

    for n, same in partners:
        part_copy(n, same).start()
    for d in range(1, n_kv):
        doc_copy(d).start()
    for g in range(GROUPS):
        send(g, 0)
    smalls[1].start()
    smalls[2].start()
    for h in range(HEADS):
        q_in(h).start()
    for d in range(1, n_kv):
        doc_arrival(d).wait_recv()
    doc_exchange(core).start()
    doc_exchange(1 - core).wait_recv()
    tail_state()
    hop(0, 0)
    masks()
    for h in range(HEADS):
        q_in(h).wait()
    smalls[1].wait()
    smalls[2].wait()
    hop(1, 0)
    hop(2, 0)
    hop(3, 0)
    part_memory()
    hop(0, 1)
    hop(1, 1)
    hop(2, 1)
    hop(3, 1)

    @pl.loop(0, HEADS // 2)
    def _(i):
        near(i)

        @pl.when(i == 0)
        def _():
            own_memory()
            hop(0, 2)

        @pl.when(i == 2)
        def _():
            hop(1, 2)

        @pl.when(i == 4)
        def _():
            hop(2, 2)

        @pl.when(i == 6)
        def _():
            hop(3, 2)

    @pl.when(me < half)
    def _():
        @pl.loop(0, HEADS // 2)
        def _(i):
            pl.when(me == half - 1)(lambda: far(i, FAR[:1]))
            pl.when(me < half - 1)(lambda: settle(i))

        for n in (3, 0, 1, 2):
            for k, same in partners:
                if k == n:
                    memory_in(k, same).wait_recv()
            recall(lax.rem(me + (GROUPS - 1, 1, 2, 0)[n], GROUPS))

    @pl.when(me >= half)
    def _():
        @pl.loop(0, GROUPS)
        def _(g):
            for ahead in range(GROUPS):
                @pl.when(g == ahead)
                def _():
                    hop(ahead, half - 1)

            @pl.loop(2 * g, 2 * g + 2)
            def _(i):
                far(i, FAR)

            @pl.when(g == 0)
            def _():
                for n, same in partners:
                    memory_in(n, same).wait_recv()

            recall(g)

    for h in range(half):
        for onward, on, whole in legs(h, 0):
            @pl.when(on)
            def _():
                for g in range(GROUPS):
                    ring(onward, g, h, 0, whole).wait_send()
    for d in range(1, n_kv):
        doc_copy(d).wait_send()
    doc_exchange(core).wait_send()
    for n, same in partners:
        part_copy(n, same).wait_send()
        memory_out(n, same).wait_send()
    state_along(1).wait_send()
    state_along(2).wait_send()
    state_across().wait_send()
    for h in range(HEADS):
        out_copy(h).wait()


def on_device(n_kv, n_seq, queries, keys, values, doc_ids, beta, lin_gain):
    rows = queries.shape[0]
    dma = pltpu.SemaphoreType.DMA
    part = D // 2
    return pl.pallas_call(
        functools.partial(kernel, n_kv, n_seq, rows),
        out_shape=jax.ShapeDtypeStruct((rows, HEADS * D), F32),
        in_specs=[pl.BlockSpec(memory_space=pltpu.HBM)] * 6,
        out_specs=pl.BlockSpec(memory_space=pl.ANY),
        scratch_shapes=[
            pltpu.VMEM((1, rows), jnp.int32),
            pltpu.SMEM((HEADS,), F32),
            pltpu.VMEM((1, HEADS * D), F32),
            pltpu.VMEM((HEADS, rows, D), BF16),
            pltpu.VMEM((GROUPS, rows, D), BF16),
            pltpu.VMEM((GROUPS, n_kv, D + rows, D), BF16),
            pltpu.VMEM((2, n_kv, 16, rows), BF16),
            pltpu.VMEM((n_kv, rows, rows), F32),
            pltpu.VMEM((HEADS // 2, 2 * rows, 1), F32),
            pltpu.VMEM((HEADS // 2, 2 * rows, 1), F32),
            pltpu.VMEM((HEADS // 2, 2 * rows, D), F32),
            pltpu.VMEM((HEADS, rows, D), F32),
            pltpu.VMEM((2 * GROUPS, part, D), F32),
            pltpu.VMEM((4, 2, part, D), F32),
            pltpu.VMEM((part + 8, D), F32),
            pltpu.VMEM((2, part + 8, D), F32),
            pltpu.VMEM((2, part, D), F32),
            pltpu.VMEM((2, part, D), F32),
            pltpu.VMEM((2, part, D), F32),
            pltpu.VMEM((2 * GROUPS, part, D), F32),
            dma((2 * GROUPS + HEADS + 3,)),
            dma((HEADS,)),
            dma((2, GROUPS, n_kv // 2)),
            dma((2, GROUPS, n_kv // 2)),
            dma((n_kv,)),
            dma((n_kv,)),
            dma((4, 2)),
            dma((4, 2)),
            dma((3,)),
            dma((3,)),
            dma((4, 2)),
            dma((4, 2)),
        ],
        compiler_params=pltpu.CompilerParams(
            collective_id=0, has_side_effects=True, vmem_limit_bytes=60 * 1024 * 1024),
    )(queries, keys, values, doc_ids.reshape(1, rows), beta, lin_gain.reshape(1, HEADS * D))


def solution(mesh):
    split = P(("dp", "seq", "kv"))
    rows = P(("dp", "seq", "kv"), None)
    return jax.shard_map(
        functools.partial(on_device, mesh.shape["kv"], mesh.shape["seq"]),
        mesh=mesh, in_specs=(rows, rows, rows, split, P(), P()), out_specs=rows, check_vma=False)
```

```python
import functools
import math

import jax
import jax.numpy as jnp
from jax import lax
from jax.experimental import pallas as pl
from jax.experimental.pallas import tpu as pltpu
from jax.sharding import PartitionSpec as P

HEADS = 16
GROUPS = 4
D = 128
MESH = pl.DeviceIdType.MESH
F32 = jnp.float32
BF16 = jnp.bfloat16
NEG = -1e30
NEAR = (-2, -1, 0, 1, 2)
BACK = (-2, -1, 0)
FAR = (-3, 3, 4)


def kernel(n_kv, n_seq, rows, q_hbm, k_hbm, v_hbm, docs_hbm, beta_hbm, gain_hbm, out_hbm,
           docs_ref, beta_ref, gain_ref, q_vm, k_vm, kv, docs, bias, top, total, acc, att, p_own, p_in, c_own, c_in, x_own, x_in, m_own, mem,
           in_sem, out_sem, ring_send, ring_recv, doc_send, doc_recv, p_send, p_recv, st_send, st_recv, mem_send, mem_recv):
    me = lax.axis_index("kv")
    seq = lax.axis_index("seq")
    core = lax.rem(seq, 2)
    other = seq + 1 - 2 * core
    chip = seq // 2
    half = n_kv // 2
    part = D // 2
    mine = 2 * lax.rem(me, GROUPS) + core
    odd_step = 4 * lax.rem(me, 2) - 2
    steps = (1, -1, odd_step, 0)

    def away(step):
        return lax.rem(me + step + n_kv, n_kv)

    def along(step):
        return lax.rem(seq + 2 * step + n_seq, n_seq)

    barrier = pltpu.get_barrier_semaphore()
    for d in range(1, n_kv):
        pl.semaphore_signal(barrier, inc=1, device_id={"kv": away(d)}, device_id_type=MESH)
    for d in (1, 2, -1, -2):
        pl.semaphore_signal(barrier, inc=1, device_id={"kv": away(d), "seq": other}, device_id_type=MESH)
    for d in (other, along(1), along(2), along(-1), along(-2)):
        pl.semaphore_signal(barrier, inc=1, device_id={"seq": d}, device_id_type=MESH)

    def k_in(g):
        return pltpu.make_async_copy(k_hbm.at[:, pl.ds(g * D, D)], k_vm.at[g], in_sem.at[g])

    def v_in(g):
        return pltpu.make_async_copy(
            v_hbm.at[:, pl.ds(g * D, D)], kv.at[g, me, pl.ds(D, rows)], in_sem.at[GROUPS + g])

    def q_in(h):
        cols = pl.ds(pl.multiple_of(h * D, D), D)
        return pltpu.make_async_copy(q_hbm.at[:, cols], q_vm.at[h], in_sem.at[2 * GROUPS + h])

    smalls = [pltpu.make_async_copy(a, b, in_sem.at[2 * GROUPS + HEADS + n]) for n, (a, b) in enumerate(
        ((docs_hbm, docs_ref), (beta_hbm, beta_ref), (gain_hbm, gain_ref)))]
    smalls[0].start()
    for g in range(GROUPS):
        k_in(g).start()
    for g in range(GROUPS):
        v_in(g).start()
    smalls[0].wait()
    docs[core, me] = jnp.broadcast_to(docs_ref[...].astype(BF16), (16, rows))
    for j in range(half, n_kv):
        @pl.when(j > me)
        def _():
            for g in range(GROUPS):
                kv[g, j] = jnp.zeros((D + rows, D), BF16)
    for g in range(GROUPS):
        k_in(g).wait()
        kv[g, me, 0:D] = k_vm[g].T
    own_row = docs_ref[...].astype(F32)
    own_last = jnp.max(own_row, axis=1, keepdims=True)
    ending = jnp.where(own_row == own_last, 1.0, 0.0).astype(BF16)
    for g in range(GROUPS):
        v_in(g).wait()
        p = jnp.dot(kv[g, me, 0:D] * ending, kv[g, me, D:D + rows], preferred_element_type=F32)
        for n in range(D // part):
            p_own[g * (D // part) + n] = p[n * part:(n + 1) * part]
    pl.semaphore_wait(barrier, n_kv - 1 + 9)

    def core_at(same):
        return (core, seq) if same else (1 - core, other)

    others = [(d, same) for d in range(n_kv) for same in (True, False) if d or not same]
    partners = [(n, same) for n in range(4) for same in (True, False) if n < 3 or not same]

    def doc_copy(d):
        ref = docs.at[core, me]
        return pltpu.make_async_remote_copy(
            src_ref=ref, dst_ref=ref, send_sem=doc_send.at[d], recv_sem=doc_recv.at[d],
            device_id={"kv": away(d)}, device_id_type=MESH)

    def doc_arrival(d):
        ref = docs.at[core, away(-d)]
        return pltpu.make_async_remote_copy(
            src_ref=ref, dst_ref=ref, send_sem=doc_send.at[d], recv_sem=doc_recv.at[d],
            device_id={"kv": away(d)}, device_id_type=MESH)

    def doc_exchange(c):
        ref = docs.at[c]
        return pltpu.make_async_remote_copy(
            src_ref=ref, dst_ref=ref, send_sem=doc_send.at[0], recv_sem=doc_recv.at[0],
            device_id={"seq": other}, device_id_type=MESH)

    def part_copy(n, same):
        c, s = core_at(same)
        to = away(steps[n])
        return pltpu.make_async_remote_copy(
            src_ref=p_own.at[2 * lax.rem(to, GROUPS) + c], dst_ref=p_in.at[n, core],
            send_sem=p_send.at[n, c], recv_sem=p_recv.at[n, core],
            device_id={"kv": to, "seq": s}, device_id_type=MESH)

    def part_arrival(n, same):
        c, s = core_at(same)
        return pltpu.make_async_remote_copy(
            src_ref=p_own.at[mine], dst_ref=p_in.at[n, c],
            send_sem=p_send.at[n, c], recv_sem=p_recv.at[n, c],
            device_id={"kv": me, "seq": other}, device_id_type=MESH)

    def span(h, onward, whole):
        if h < half - 1 and whole:
            return pl.ds(0, D + rows)
        return pl.ds(0, D) if onward else pl.ds(D, rows)

    def ring(onward, g, h, ahead, whole=True):
        blk = away(-h - ahead if onward else h + ahead)
        ref = kv.at[g, blk, span(h, onward, whole)]
        t = 0 if onward else 1
        return pltpu.make_async_remote_copy(
            src_ref=ref, dst_ref=ref, send_sem=ring_send.at[t, g, h], recv_sem=ring_recv.at[t, g, h],
            device_id={"kv": away(1 if onward else -1)}, device_id_type=MESH)

    def legs(h, ahead):
        right_on = (me >= h) & (me < n_kv - 1) if ahead == 0 else me > h
        blk = away(h + ahead)
        if h == half - 1:
            return ((True, right_on, True), (False, blk < half, True))
        return ((True, right_on, True), (False, blk < half - 1, True), (False, blk == half - 1, False))

    def send(g, h):
        for onward, on, whole in legs(h, 0):
            @pl.when(on)
            def _():
                ring(onward, g, h, 0, whole).start()

    def hop(g, h):
        for onward, on, whole in legs(h, 1):
            @pl.when(on)
            def _():
                ring(onward, g, h, 1, whole).wait_recv()
        if h + 1 < half:
            send(g, h + 1)

    def state_along(step):
        return pltpu.make_async_remote_copy(
            src_ref=c_own, dst_ref=c_in.at[step - 1], send_sem=st_send.at[step - 1], recv_sem=st_recv.at[step - 1],
            device_id={"seq": along(step)}, device_id_type=MESH)

    def state_across():
        return pltpu.make_async_remote_copy(
            src_ref=x_own, dst_ref=x_in, send_sem=st_send.at[2], recv_sem=st_recv.at[2],
            device_id={"kv": away(half)}, device_id_type=MESH)

    def memory_out(n, same):
        c, s = core_at(same)
        return pltpu.make_async_remote_copy(
            src_ref=m_own.at[c], dst_ref=mem.at[mine],
            send_sem=mem_send.at[n, c], recv_sem=mem_recv.at[n, core],
            device_id={"kv": away(steps[n]), "seq": s}, device_id_type=MESH)

    def memory_in(n, same):
        c, s = core_at(same)
        g = lax.rem(me + (GROUPS - 1, 1, 2, 0)[n], GROUPS)
        return pltpu.make_async_remote_copy(
            src_ref=m_own.at[c], dst_ref=mem.at[2 * g + c], send_sem=mem_send.at[n, c], recv_sem=mem_recv.at[n, c],
            device_id={"kv": me, "seq": other}, device_id_type=MESH)

    own_doc = jnp.broadcast_to(own_row, (rows, rows)).T

    def doc_row(j, c=None):
        return docs[core if c is None else c, j].astype(F32)[0:1]

    def ends():
        last = jnp.max(doc_row(n_kv - 1), axis=1, keepdims=True)
        first = jnp.min(doc_row(0), axis=1, keepdims=True)
        return first, last

    def masks():
        row = lax.broadcasted_iota(jnp.int32, (rows, rows), 0)
        lane = lax.broadcasted_iota(jnp.int32, (rows, rows), 1)
        for j in range(n_kv):
            allowed = (doc_row(j) == own_doc) & (j * rows + lane <= me * rows + row)
            bias[j] = jnp.where(allowed, 0.0, NEG)

    scale = math.log2(math.e) / math.sqrt(D)

    def mixing(h):
        return jax.nn.sigmoid(jnp.full((1, D), beta_ref[h], F32))

    def scores(i, offs):
        g = i // 2
        q2 = jnp.concatenate([q_vm[2 * i], q_vm[2 * i + 1]], axis=0)
        kt = jnp.concatenate([kv[g, away(o), 0:D] for o in offs], axis=1)
        b = jnp.concatenate([bias[away(o)] for o in offs], axis=1)
        s = jnp.dot(q2, kt, preferred_element_type=F32)
        return s + jnp.concatenate([b, b], axis=0)

    def weighted(i, offs, p):
        v = jnp.concatenate([kv[i // 2, away(o), D:D + rows] for o in offs], axis=0)
        return jnp.dot(p.astype(BF16), v, preferred_element_type=F32)

    def first_pass(i, offs):
        s = scores(i, offs)
        m = jnp.max(s, axis=-1, keepdims=True)
        p = jnp.exp2((s - m) * scale)
        top[i] = m
        total[i] = jnp.sum(p, axis=-1, keepdims=True)
        acc[i] = weighted(i, offs, p)

    def near(i):
        pl.when(me < n_kv - 2)(lambda: first_pass(i, BACK))
        pl.when(me >= n_kv - 2)(lambda: first_pass(i, NEAR))

    def far(i, offs):
        s = scores(i, offs)
        old = top[i]
        m = jnp.maximum(old, jnp.max(s, axis=-1, keepdims=True))
        p = jnp.exp2((s - m) * scale)
        kept = jnp.exp2((old - m) * scale)
        norm = total[i] * kept + jnp.sum(p, axis=-1, keepdims=True)
        o = (acc[i] * kept + weighted(i, offs, p)) / norm
        att[2 * i] = o[:rows] * (1.0 - mixing(2 * i))
        att[2 * i + 1] = o[rows:] * (1.0 - mixing(2 * i + 1))

    def settle(i):
        o = acc[i] / total[i]
        att[2 * i] = o[:rows] * (1.0 - mixing(2 * i))
        att[2 * i + 1] = o[rows:] * (1.0 - mixing(2 * i + 1))

    def some(f, start, stop):
        pl.loop(start, stop)(f)

    def edges(c):
        last = jnp.max(doc_row(n_kv - 1, c), axis=1, keepdims=True)
        first = jnp.min(doc_row(0, c), axis=1, keepdims=True)
        return first, last

    def tail_state():
        p_in[3, core] = p_own[mine]
        for n, same in partners:
            part_arrival(n, same).wait_recv()
        states = []
        for c in range(2):
            first, last = edges(c)

            def counted(n):
                here = jnp.max(doc_row(away(-steps[n]), c), axis=1, keepdims=True)
                return jnp.where(here == last, p_in[n, c], 0.0)

            states.append((sum(counted(n) for n in range(4)), first, last))
        (even, _, even_last), (odd, odd_first, odd_last) = states
        c_own[0:part] = odd + jnp.where(even_last == odd_last, even, 0.0)
        c_own[part:part + 8] = jnp.broadcast_to(odd_last, (8, D))
        state_along(1).start()
        state_along(2).start()
        x_own[1] = jnp.where(even_last == odd_first, even, 0.0)

    def part_memory():
        state_along(1).wait_recv()
        state_along(2).wait_recv()
        one, two = c_in[0], c_in[1]
        for c in range(2):
            first = edges(c)[0]
            m = jnp.where((one[part:part + 1] == first) & (chip >= 1), one[0:part], 0.0)
            m = m + jnp.where((two[part:part + 1] == first) & (chip >= 2), two[0:part], 0.0)
            x_own[c] = m + x_own[1] if c else m
        state_across().start()

    def own_memory():
        state_across().wait_recv()
        m_own[...] = x_own[...] + x_in[...]
        mem[mine] = x_own[core] + x_in[core]
        for n, same in partners:
            memory_out(n, same).start()

    def out_copy(h):
        cols = pl.ds(pl.multiple_of(h * D, D), D)
        return pltpu.make_async_copy(att.at[h], out_hbm.at[:, cols], out_sem.at[h])

    def recall(g):
        live = jnp.where(own_doc[:, 0:1] == ends()[0], 1.0, 0.0)
        state = jnp.concatenate([mem[g * (D // part) + n] for n in range(D // part)], axis=0)
        hi = state.astype(BF16)
        lo = (state - hi.astype(F32)).astype(BF16)
        both = jnp.concatenate([hi, lo], axis=1)
        q4 = jnp.concatenate([q_vm[4 * g + k] for k in range(4)], axis=0)
        r = jnp.dot(q4, both, preferred_element_type=F32)
        r = r[:, 0:D] + r[:, D:]
        for k in range(4):
            h = 4 * g + k
            rh = r[k * rows:(k + 1) * rows] * live
            mean = jnp.mean(rh * rh, axis=-1, keepdims=True)
            cols = pl.ds(pl.multiple_of(h * D, D), D)
            att[h] = att[h] + rh * lax.rsqrt(mean + 1e-6) * (gain_ref[:, cols] * mixing(h))
            out_copy(h).start()

    for n, same in partners:
        part_copy(n, same).start()
    for d in range(1, n_kv):
        doc_copy(d).start()
    for g in range(GROUPS):
        send(g, 0)
    smalls[1].start()
    smalls[2].start()
    for h in range(HEADS):
        q_in(h).start()
    for d in range(1, n_kv):
        doc_arrival(d).wait_recv()
    doc_exchange(core).start()
    doc_exchange(1 - core).wait_recv()
    tail_state()
    hop(0, 0)
    masks()
    for h in range(HEADS):
        q_in(h).wait()
    smalls[1].wait()
    smalls[2].wait()
    hop(1, 0)
    hop(2, 0)
    hop(3, 0)
    part_memory()
    hop(0, 1)
    hop(1, 1)
    hop(2, 1)
    hop(3, 1)

    @pl.loop(0, HEADS // 2)
    def _(i):
        near(i)

        @pl.when(i == 0)
        def _():
            hop(0, 2)
            own_memory()

        @pl.when(i == 2)
        def _():
            hop(1, 2)

        @pl.when(i == 4)
        def _():
            hop(2, 2)

        @pl.when(i == 6)
        def _():
            hop(3, 2)

    @pl.when(me < half)
    def _():
        @pl.loop(0, HEADS // 2)
        def _(i):
            pl.when(me == half - 1)(lambda: far(i, FAR[:1]))
            pl.when(me < half - 1)(lambda: settle(i))

        for n in (3, 0, 1, 2):
            for k, same in partners:
                if k == n:
                    memory_in(k, same).wait_recv()
            recall(lax.rem(me + (GROUPS - 1, 1, 2, 0)[n], GROUPS))

    @pl.when(me >= half)
    def _():
        @pl.loop(0, GROUPS)
        def _(g):
            for ahead in range(GROUPS):
                @pl.when(g == ahead)
                def _():
                    hop(ahead, half - 1)

            @pl.loop(2 * g, 2 * g + 2)
            def _(i):
                pl.when(me == half)(lambda: far(i, FAR[::2]))
                pl.when(me > half)(lambda: far(i, FAR))

            @pl.when(g == 0)
            def _():
                for n, same in partners:
                    memory_in(n, same).wait_recv()

            recall(g)

    for h in range(half):
        for onward, on, whole in legs(h, 0):
            @pl.when(on)
            def _():
                for g in range(GROUPS):
                    ring(onward, g, h, 0, whole).wait_send()
    for d in range(1, n_kv):
        doc_copy(d).wait_send()
    doc_exchange(core).wait_send()
    for n, same in partners:
        part_copy(n, same).wait_send()
        memory_out(n, same).wait_send()
    state_along(1).wait_send()
    state_along(2).wait_send()
    state_across().wait_send()
    for h in range(HEADS):
        out_copy(h).wait()


def on_device(n_kv, n_seq, queries, keys, values, doc_ids, beta, lin_gain):
    rows = queries.shape[0]
    dma = pltpu.SemaphoreType.DMA
    part = D // 2
    return pl.pallas_call(
        functools.partial(kernel, n_kv, n_seq, rows),
        out_shape=jax.ShapeDtypeStruct((rows, HEADS * D), F32),
        in_specs=[pl.BlockSpec(memory_space=pltpu.HBM)] * 6,
        out_specs=pl.BlockSpec(memory_space=pl.ANY),
        scratch_shapes=[
            pltpu.VMEM((1, rows), jnp.int32),
            pltpu.SMEM((HEADS,), F32),
            pltpu.VMEM((1, HEADS * D), F32),
            pltpu.VMEM((HEADS, rows, D), BF16),
            pltpu.VMEM((GROUPS, rows, D), BF16),
            pltpu.VMEM((GROUPS, n_kv, D + rows, D), BF16),
            pltpu.VMEM((2, n_kv, 16, rows), BF16),
            pltpu.VMEM((n_kv, rows, rows), F32),
            pltpu.VMEM((HEADS // 2, 2 * rows, 1), F32),
            pltpu.VMEM((HEADS // 2, 2 * rows, 1), F32),
            pltpu.VMEM((HEADS // 2, 2 * rows, D), F32),
            pltpu.VMEM((HEADS, rows, D), F32),
            pltpu.VMEM((2 * GROUPS, part, D), F32),
            pltpu.VMEM((4, 2, part, D), F32),
            pltpu.VMEM((part + 8, D), F32),
            pltpu.VMEM((2, part + 8, D), F32),
            pltpu.VMEM((2, part, D), F32),
            pltpu.VMEM((2, part, D), F32),
            pltpu.VMEM((2, part, D), F32),
            pltpu.VMEM((2 * GROUPS, part, D), F32),
            dma((2 * GROUPS + HEADS + 3,)),
            dma((HEADS,)),
            dma((2, GROUPS, n_kv // 2)),
            dma((2, GROUPS, n_kv // 2)),
            dma((n_kv,)),
            dma((n_kv,)),
            dma((4, 2)),
            dma((4, 2)),
            dma((3,)),
            dma((3,)),
            dma((4, 2)),
            dma((4, 2)),
        ],
        compiler_params=pltpu.CompilerParams(
            collective_id=0, has_side_effects=True, vmem_limit_bytes=60 * 1024 * 1024),
    )(queries, keys, values, doc_ids.reshape(1, rows), beta, lin_gain.reshape(1, HEADS * D))


def solution(mesh):
    split = P(("dp", "seq", "kv"))
    rows = P(("dp", "seq", "kv"), None)
    return jax.shard_map(
        functools.partial(on_device, mesh.shape["kv"], mesh.shape["seq"]),
        mesh=mesh, in_specs=(rows, rows, rows, split, P(), P()), out_specs=rows, check_vma=False)
```

```python
import functools
import math

import jax
import jax.numpy as jnp
from jax import lax
from jax.experimental import pallas as pl
from jax.experimental.pallas import tpu as pltpu
from jax.sharding import PartitionSpec as P

HEADS = 16
GROUPS = 4
D = 128
MESH = pl.DeviceIdType.MESH
F32 = jnp.float32
BF16 = jnp.bfloat16
NEG = -1e30
NEAR = (-2, -1, 0, 1, 2)
BACK = (-2, -1, 0)
FAR = (-3, 3, 4)


def kernel(n_kv, n_seq, rows, q_hbm, k_hbm, v_hbm, docs_hbm, beta_hbm, gain_hbm, out_hbm,
           docs_ref, beta_ref, gain_ref, q_vm, k_vm, kv, docs, bias, top, total, acc, att, p_own, p_in, c_own, c_in, x_own, x_in, m_own, mem,
           in_sem, out_sem, ring_send, ring_recv, doc_send, doc_recv, p_send, p_recv, st_send, st_recv, mem_send, mem_recv):
    me = lax.axis_index("kv")
    seq = lax.axis_index("seq")
    core = lax.rem(seq, 2)
    other = seq + 1 - 2 * core
    chip = seq // 2
    half = n_kv // 2
    part = D // 2
    mine = 2 * lax.rem(me, GROUPS) + core
    odd_step = 4 * lax.rem(me, 2) - 2
    steps = (1, -1, odd_step, 0)

    def away(step):
        return lax.rem(me + step + n_kv, n_kv)

    def along(step):
        return lax.rem(seq + 2 * step + n_seq, n_seq)

    barrier = pltpu.get_barrier_semaphore()
    for d in range(1, n_kv):
        pl.semaphore_signal(barrier, inc=1, device_id={"kv": away(d)}, device_id_type=MESH)
    for d in (1, 2, -1, -2):
        pl.semaphore_signal(barrier, inc=1, device_id={"kv": away(d), "seq": other}, device_id_type=MESH)
    for d in (other, along(1), along(2), along(-1), along(-2)):
        pl.semaphore_signal(barrier, inc=1, device_id={"seq": d}, device_id_type=MESH)

    def k_in(g):
        return pltpu.make_async_copy(k_hbm.at[:, pl.ds(g * D, D)], k_vm.at[g], in_sem.at[g])

    def v_in(g):
        return pltpu.make_async_copy(
            v_hbm.at[:, pl.ds(g * D, D)], kv.at[g, me, pl.ds(D, rows)], in_sem.at[GROUPS + g])

    def q_in(h):
        cols = pl.ds(pl.multiple_of(h * D, D), D)
        return pltpu.make_async_copy(q_hbm.at[:, cols], q_vm.at[h], in_sem.at[2 * GROUPS + h])

    smalls = [pltpu.make_async_copy(a, b, in_sem.at[2 * GROUPS + HEADS + n]) for n, (a, b) in enumerate(
        ((docs_hbm, docs_ref), (beta_hbm, beta_ref), (gain_hbm, gain_ref)))]
    smalls[0].start()
    for g in range(GROUPS):
        k_in(g).start()
    for g in range(GROUPS):
        v_in(g).start()
    smalls[0].wait()
    docs[core, me] = jnp.broadcast_to(docs_ref[...].astype(BF16), (16, rows))
    for j in range(half, n_kv):
        @pl.when(j > me)
        def _():
            for g in range(GROUPS):
                kv[g, j] = jnp.zeros((D + rows, D), BF16)
    for g in range(GROUPS):
        k_in(g).wait()
        kv[g, me, 0:D] = k_vm[g].T
    own_row = docs_ref[...].astype(F32)
    own_last = jnp.max(own_row, axis=1, keepdims=True)
    ending = jnp.where(own_row == own_last, 1.0, 0.0).astype(BF16)
    for g in range(GROUPS):
        v_in(g).wait()
        p = jnp.dot(kv[g, me, 0:D] * ending, kv[g, me, D:D + rows], preferred_element_type=F32)
        for n in range(D // part):
            p_own[g * (D // part) + n] = p[n * part:(n + 1) * part]
    pl.semaphore_wait(barrier, n_kv - 1 + 9)

    def core_at(same):
        return (core, seq) if same else (1 - core, other)

    others = [(d, same) for d in range(n_kv) for same in (True, False) if d or not same]
    partners = [(n, same) for n in (2, 0, 1, 3) for same in (True, False) if n < 3 or not same]

    def doc_copy(d):
        ref = docs.at[core, me]
        return pltpu.make_async_remote_copy(
            src_ref=ref, dst_ref=ref, send_sem=doc_send.at[d], recv_sem=doc_recv.at[d],
            device_id={"kv": away(d)}, device_id_type=MESH)

    def doc_arrival(d):
        ref = docs.at[core, away(-d)]
        return pltpu.make_async_remote_copy(
            src_ref=ref, dst_ref=ref, send_sem=doc_send.at[d], recv_sem=doc_recv.at[d],
            device_id={"kv": away(d)}, device_id_type=MESH)

    def doc_exchange(c):
        ref = docs.at[c]
        return pltpu.make_async_remote_copy(
            src_ref=ref, dst_ref=ref, send_sem=doc_send.at[0], recv_sem=doc_recv.at[0],
            device_id={"seq": other}, device_id_type=MESH)

    def part_copy(n, same):
        c, s = core_at(same)
        to = away(steps[n])
        return pltpu.make_async_remote_copy(
            src_ref=p_own.at[2 * lax.rem(to, GROUPS) + c], dst_ref=p_in.at[n, core],
            send_sem=p_send.at[n, c], recv_sem=p_recv.at[n, core],
            device_id={"kv": to, "seq": s}, device_id_type=MESH)

    def part_arrival(n, same):
        c, s = core_at(same)
        return pltpu.make_async_remote_copy(
            src_ref=p_own.at[mine], dst_ref=p_in.at[n, c],
            send_sem=p_send.at[n, c], recv_sem=p_recv.at[n, c],
            device_id={"kv": me, "seq": other}, device_id_type=MESH)

    def span(h, onward, whole):
        if h < half - 1 and whole:
            return pl.ds(0, D + rows)
        return pl.ds(0, D) if onward else pl.ds(D, rows)

    def ring(onward, g, h, ahead, whole=True):
        blk = away(-h - ahead if onward else h + ahead)
        ref = kv.at[g, blk, span(h, onward, whole)]
        t = 0 if onward else 1
        return pltpu.make_async_remote_copy(
            src_ref=ref, dst_ref=ref, send_sem=ring_send.at[t, g, h], recv_sem=ring_recv.at[t, g, h],
            device_id={"kv": away(1 if onward else -1)}, device_id_type=MESH)

    def legs(h, ahead):
        right_on = (me >= h) & (me < n_kv - 1) if ahead == 0 else me > h
        blk = away(h + ahead)
        if h == half - 1:
            return ((True, right_on, True), (False, blk < half, True))
        return ((True, right_on, True), (False, blk < half - 1, True), (False, blk == half - 1, False))

    def send(g, h):
        for onward, on, whole in legs(h, 0):
            @pl.when(on)
            def _():
                ring(onward, g, h, 0, whole).start()

    def hop(g, h):
        for onward, on, whole in legs(h, 1):
            @pl.when(on)
            def _():
                ring(onward, g, h, 1, whole).wait_recv()
        if h + 1 < half:
            send(g, h + 1)

    def state_along(step):
        return pltpu.make_async_remote_copy(
            src_ref=c_own, dst_ref=c_in.at[step - 1], send_sem=st_send.at[step - 1], recv_sem=st_recv.at[step - 1],
            device_id={"seq": along(step)}, device_id_type=MESH)

    def state_across():
        return pltpu.make_async_remote_copy(
            src_ref=x_own, dst_ref=x_in, send_sem=st_send.at[2], recv_sem=st_recv.at[2],
            device_id={"kv": away(half)}, device_id_type=MESH)

    def memory_out(n, same):
        c, s = core_at(same)
        return pltpu.make_async_remote_copy(
            src_ref=m_own.at[c], dst_ref=mem.at[mine],
            send_sem=mem_send.at[n, c], recv_sem=mem_recv.at[n, core],
            device_id={"kv": away(steps[n]), "seq": s}, device_id_type=MESH)

    def memory_in(n, same):
        c, s = core_at(same)
        g = lax.rem(me + (GROUPS - 1, 1, 2, 0)[n], GROUPS)
        return pltpu.make_async_remote_copy(
            src_ref=m_own.at[c], dst_ref=mem.at[2 * g + c], send_sem=mem_send.at[n, c], recv_sem=mem_recv.at[n, c],
            device_id={"kv": me, "seq": other}, device_id_type=MESH)

    own_doc = jnp.broadcast_to(own_row, (rows, rows)).T

    def doc_row(j, c=None):
        return docs[core if c is None else c, j].astype(F32)[0:1]

    def ends():
        last = jnp.max(doc_row(n_kv - 1), axis=1, keepdims=True)
        first = jnp.min(doc_row(0), axis=1, keepdims=True)
        return first, last

    def masks():
        row = lax.broadcasted_iota(jnp.int32, (rows, rows), 0)
        lane = lax.broadcasted_iota(jnp.int32, (rows, rows), 1)
        for j in range(n_kv):
            allowed = (doc_row(j) == own_doc) & (j * rows + lane <= me * rows + row)
            bias[j] = jnp.where(allowed, 0.0, NEG)

    scale = math.log2(math.e) / math.sqrt(D)

    def mixing(h):
        return jax.nn.sigmoid(jnp.full((1, D), beta_ref[h], F32))

    def scores(i, offs):
        g = i // 2
        q2 = jnp.concatenate([q_vm[2 * i], q_vm[2 * i + 1]], axis=0)
        kt = jnp.concatenate([kv[g, away(o), 0:D] for o in offs], axis=1)
        b = jnp.concatenate([bias[away(o)] for o in offs], axis=1)
        s = jnp.dot(q2, kt, preferred_element_type=F32)
        return s + jnp.concatenate([b, b], axis=0)

    def weighted(i, offs, p):
        v = jnp.concatenate([kv[i // 2, away(o), D:D + rows] for o in offs], axis=0)
        return jnp.dot(p.astype(BF16), v, preferred_element_type=F32)

    def first_pass(i, offs):
        s = scores(i, offs)
        m = jnp.max(s, axis=-1, keepdims=True)
        p = jnp.exp2((s - m) * scale)
        top[i] = m
        total[i] = jnp.sum(p, axis=-1, keepdims=True)
        acc[i] = weighted(i, offs, p)

    def near(i):
        pl.when(me < n_kv - 2)(lambda: first_pass(i, BACK))
        pl.when(me >= n_kv - 2)(lambda: first_pass(i, NEAR))

    def far(i, offs):
        s = scores(i, offs)
        old = top[i]
        m = jnp.maximum(old, jnp.max(s, axis=-1, keepdims=True))
        p = jnp.exp2((s - m) * scale)
        kept = jnp.exp2((old - m) * scale)
        norm = total[i] * kept + jnp.sum(p, axis=-1, keepdims=True)
        o = (acc[i] * kept + weighted(i, offs, p)) / norm
        att[2 * i] = o[:rows] * (1.0 - mixing(2 * i))
        att[2 * i + 1] = o[rows:] * (1.0 - mixing(2 * i + 1))

    def settle(i):
        o = acc[i] / total[i]
        att[2 * i] = o[:rows] * (1.0 - mixing(2 * i))
        att[2 * i + 1] = o[rows:] * (1.0 - mixing(2 * i + 1))

    def some(f, start, stop):
        pl.loop(start, stop)(f)

    def edges(c):
        last = jnp.max(doc_row(n_kv - 1, c), axis=1, keepdims=True)
        first = jnp.min(doc_row(0, c), axis=1, keepdims=True)
        return first, last

    def tail_state():
        p_in[3, core] = p_own[mine]
        for n, same in partners:
            part_arrival(n, same).wait_recv()
        states = []
        for c in range(2):
            first, last = edges(c)

            def counted(n):
                here = jnp.max(doc_row(away(-steps[n]), c), axis=1, keepdims=True)
                return jnp.where(here == last, p_in[n, c], 0.0)

            states.append((sum(counted(n) for n in range(4)), first, last))
        (even, _, even_last), (odd, odd_first, odd_last) = states
        c_own[0:part] = odd + jnp.where(even_last == odd_last, even, 0.0)
        c_own[part:part + 8] = jnp.broadcast_to(odd_last, (8, D))
        state_along(2).start()
        state_along(1).start()
        x_own[1] = jnp.where(even_last == odd_first, even, 0.0)

    def part_memory():
        state_along(1).wait_recv()
        state_along(2).wait_recv()
        one, two = c_in[0], c_in[1]
        for c in range(2):
            first = edges(c)[0]
            m = jnp.where((one[part:part + 1] == first) & (chip >= 1), one[0:part], 0.0)
            m = m + jnp.where((two[part:part + 1] == first) & (chip >= 2), two[0:part], 0.0)
            x_own[c] = m + x_own[1] if c else m
        state_across().start()

    def own_memory():
        state_across().wait_recv()
        m_own[...] = x_own[...] + x_in[...]
        mem[mine] = x_own[core] + x_in[core]
        for n, same in partners:
            memory_out(n, same).start()

    def out_copy(h):
        cols = pl.ds(pl.multiple_of(h * D, D), D)
        return pltpu.make_async_copy(att.at[h], out_hbm.at[:, cols], out_sem.at[h])

    def recall(g):
        live = jnp.where(own_doc[:, 0:1] == ends()[0], 1.0, 0.0)
        state = jnp.concatenate([mem[g * (D // part) + n] for n in range(D // part)], axis=0)
        hi = state.astype(BF16)
        lo = (state - hi.astype(F32)).astype(BF16)
        both = jnp.concatenate([hi, lo], axis=1)
        q4 = jnp.concatenate([q_vm[4 * g + k] for k in range(4)], axis=0)
        r = jnp.dot(q4, both, preferred_element_type=F32)
        r = r[:, 0:D] + r[:, D:]
        for k in range(4):
            h = 4 * g + k
            rh = r[k * rows:(k + 1) * rows] * live
            mean = jnp.mean(rh * rh, axis=-1, keepdims=True)
            cols = pl.ds(pl.multiple_of(h * D, D), D)
            att[h] = att[h] + rh * lax.rsqrt(mean + 1e-6) * (gain_ref[:, cols] * mixing(h))
            out_copy(h).start()

    for n, same in partners:
        part_copy(n, same).start()
    for d in range(1, n_kv):
        doc_copy(d).start()
    for g in range(GROUPS):
        send(g, 0)
    smalls[1].start()
    smalls[2].start()
    for h in range(HEADS):
        q_in(h).start()
    for d in range(1, n_kv):
        doc_arrival(d).wait_recv()
    doc_exchange(core).start()
    doc_exchange(1 - core).wait_recv()
    tail_state()
    hop(0, 0)
    masks()
    for h in range(HEADS):
        q_in(h).wait()
    smalls[1].wait()
    smalls[2].wait()
    hop(1, 0)
    hop(2, 0)
    hop(3, 0)
    part_memory()
    hop(0, 1)
    hop(1, 1)
    hop(2, 1)
    hop(3, 1)

    @pl.loop(0, HEADS // 2)
    def _(i):
        near(i)

        @pl.when(i == 0)
        def _():
            hop(0, 2)
            own_memory()

        @pl.when(i == 2)
        def _():
            hop(1, 2)

        @pl.when(i == 4)
        def _():
            hop(2, 2)

        @pl.when(i == 6)
        def _():
            hop(3, 2)

    @pl.when(me < half)
    def _():
        @pl.loop(0, HEADS // 2)
        def _(i):
            pl.when(me == half - 1)(lambda: far(i, FAR[:1]))
            pl.when(me < half - 1)(lambda: settle(i))

        for n in (3, 0, 1, 2):
            for k, same in partners:
                if k == n:
                    memory_in(k, same).wait_recv()
            recall(lax.rem(me + (GROUPS - 1, 1, 2, 0)[n], GROUPS))

    @pl.when(me >= half)
    def _():
        @pl.loop(0, GROUPS)
        def _(g):
            for ahead in range(GROUPS):
                @pl.when(g == ahead)
                def _():
                    hop(ahead, half - 1)

            @pl.loop(2 * g, 2 * g + 2)
            def _(i):
                pl.when(me == half)(lambda: far(i, FAR[::2]))
                pl.when(me > half)(lambda: far(i, FAR))

            @pl.when(g == 0)
            def _():
                for n, same in partners:
                    memory_in(n, same).wait_recv()

            recall(g)

    for h in range(half):
        for onward, on, whole in legs(h, 0):
            @pl.when(on)
            def _():
                for g in range(GROUPS):
                    ring(onward, g, h, 0, whole).wait_send()
    for d in range(1, n_kv):
        doc_copy(d).wait_send()
    doc_exchange(core).wait_send()
    for n, same in partners:
        part_copy(n, same).wait_send()
        memory_out(n, same).wait_send()
    state_along(1).wait_send()
    state_along(2).wait_send()
    state_across().wait_send()
    for h in range(HEADS):
        out_copy(h).wait()


def on_device(n_kv, n_seq, queries, keys, values, doc_ids, beta, lin_gain):
    rows = queries.shape[0]
    dma = pltpu.SemaphoreType.DMA
    part = D // 2
    return pl.pallas_call(
        functools.partial(kernel, n_kv, n_seq, rows),
        out_shape=jax.ShapeDtypeStruct((rows, HEADS * D), F32),
        in_specs=[pl.BlockSpec(memory_space=pltpu.HBM)] * 6,
        out_specs=pl.BlockSpec(memory_space=pl.ANY),
        scratch_shapes=[
            pltpu.VMEM((1, rows), jnp.int32),
            pltpu.SMEM((HEADS,), F32),
            pltpu.VMEM((1, HEADS * D), F32),
            pltpu.VMEM((HEADS, rows, D), BF16),
            pltpu.VMEM((GROUPS, rows, D), BF16),
            pltpu.VMEM((GROUPS, n_kv, D + rows, D), BF16),
            pltpu.VMEM((2, n_kv, 16, rows), BF16),
            pltpu.VMEM((n_kv, rows, rows), F32),
            pltpu.VMEM((HEADS // 2, 2 * rows, 1), F32),
            pltpu.VMEM((HEADS // 2, 2 * rows, 1), F32),
            pltpu.VMEM((HEADS // 2, 2 * rows, D), F32),
            pltpu.VMEM((HEADS, rows, D), F32),
            pltpu.VMEM((2 * GROUPS, part, D), F32),
            pltpu.VMEM((4, 2, part, D), F32),
            pltpu.VMEM((part + 8, D), F32),
            pltpu.VMEM((2, part + 8, D), F32),
            pltpu.VMEM((2, part, D), F32),
            pltpu.VMEM((2, part, D), F32),
            pltpu.VMEM((2, part, D), F32),
            pltpu.VMEM((2 * GROUPS, part, D), F32),
            dma((2 * GROUPS + HEADS + 3,)),
            dma((HEADS,)),
            dma((2, GROUPS, n_kv // 2)),
            dma((2, GROUPS, n_kv // 2)),
            dma((n_kv,)),
            dma((n_kv,)),
            dma((4, 2)),
            dma((4, 2)),
            dma((3,)),
            dma((3,)),
            dma((4, 2)),
            dma((4, 2)),
        ],
        compiler_params=pltpu.CompilerParams(
            collective_id=0, has_side_effects=True, vmem_limit_bytes=60 * 1024 * 1024),
    )(queries, keys, values, doc_ids.reshape(1, rows), beta, lin_gain.reshape(1, HEADS * D))


def solution(mesh):
    split = P(("dp", "seq", "kv"))
    rows = P(("dp", "seq", "kv"), None)
    return jax.shard_map(
        functools.partial(on_device, mesh.shape["kv"], mesh.shape["seq"]),
        mesh=mesh, in_specs=(rows, rows, rows, split, P(), P()), out_specs=rows, check_vma=False)
```
